128 devices in a mesh: gx: 8 (over y, z_lo), gy: 16 (over x, z_hi, core).
Axes of the slice: x: 4, y: 4, z: 4 (z_hi: 2, z_lo: 2; z = z_hi * 2 + z_lo), core: 2. Of those that a mesh axis runs over, the one named last changes fastest.
Arguments:
- coef: bfloat16 [131072, 512], P(('gx', 'gy')), may hold values from -6 to 6
- tables: bfloat16 [16, 512, 512], replicated, may hold values from -0.09375 to 0.09375
- leaf_level: int32 [131072], P(('gx', 'gy')), may hold values from 0 to 2
- inner_list: int32 [131072, 8], P(('gx', 'gy')), may hold values from 0 to 131071, as said below
- inner_class: int32 [131072, 8], P(('gx', 'gy')), may hold values from 0 to 15, as said below
- cross_pairs: int32 [3, 32768], P(None, ('gx', 'gy')), may hold values from 0 to 130175, as said below
Outputs:
- potential: float32 [131072, 512], P(('gx', 'gy'))
The draws below stay inside these ranges and needn't reach their ends.
Inputs may be any that keep to these rules, and one draw needn't show every extreme that they name: `inner_list`: every entry of a row names a leaf of the same brick as the row's leaf; bricks are runs of 1024 leaves, brick number bx * 16 + by for brick column (bx, by). `inner_class`: the 8 classes of one row differ. `cross_pairs`: pair p belongs to owner brick p // 256; its target leaf is one of the first 128 leaves of the owner brick, its source one of the first 128 leaves of one of the up to eight bricks whose column differs from the owner's by at most one along x and y and which is not the owner; its class lies in 0 to 15.
All inputs are finite; a program needn't handle non-finite values.
Results may differ from the reference program's by a relative error of at most 0.0003.
Values may be sent and summed in bfloat16 or wider, within the bound.
A program may use at most 128 MiB of HBM per device.

```python
import jax
import jax.numpy as jnp
from jax import lax

NC = 512
CLASSES = 16
KNEAR = 8
LEAF_DEV = 1024
BORDER = 128
CROSS_DEV = 256
BRICKS_X = 8
BRICKS_Y = 16
LEAVES = 131072
PAIRS = 32768


def draw_inner_list(key, part):
    local = jax.random.randint(key, (LEAVES, KNEAR), 0, LEAF_DEV)
    base = (jnp.arange(LEAVES) // LEAF_DEV * LEAF_DEV)[:, None]
    result = (local + base).astype(jnp.int32)
    result = result.at[0, 0].set(0)
    result = result.at[LEAVES - 1, 0].set(LEAVES - 1)
    return result.astype(jnp.int32)


def draw_inner_class(key, part):
    scores = jax.random.randint(key, (LEAVES, CLASSES), 0, 2 ** 20) * CLASSES + jnp.arange(CLASSES)
    order = jnp.argsort(scores, axis=1)
    return order[:, :KNEAR].astype(jnp.int32)


def draw_cross_pairs(key, part):
    owner = jnp.arange(PAIRS) // CROSS_DEV
    owner_x = owner // BRICKS_Y
    owner_y = owner % BRICKS_Y
    pick = jax.random.randint(jax.random.fold_in(key, 11), (PAIRS,), 0, 8)
    pick = pick + (pick >= 4).astype(pick.dtype)
    step_x = pick // 3 - 1
    step_y = pick % 3 - 1
    next_x = jnp.where((owner_x + step_x < 0) | (owner_x + step_x >= BRICKS_X), owner_x - step_x, owner_x + step_x)
    next_y = jnp.where((owner_y + step_y < 0) | (owner_y + step_y >= BRICKS_Y), owner_y - step_y, owner_y + step_y)
    target = owner * LEAF_DEV + jax.random.randint(jax.random.fold_in(key, 12), (PAIRS,), 0, BORDER)
    target = target.at[PAIRS - 1].set(LEAVES - LEAF_DEV + BORDER - 1)
    source = (next_x * BRICKS_Y + next_y) * LEAF_DEV + jax.random.randint(jax.random.fold_in(key, 13), (PAIRS,), 0, BORDER)
    kinds = jax.random.randint(jax.random.fold_in(key, 14), (PAIRS,), 0, CLASSES)
    kinds = kinds.at[0].set(0)
    return jnp.stack([target, source, kinds]).astype(jnp.int32)


def touch_ends(drawn, rng, low, high):
    shape = drawn.shape
    place = [jax.random.randint(jax.random.fold_in(rng, axis), (), 0, shape[axis]) for axis in range(len(shape))]
    drawn = drawn.at[tuple(place)].set(low)
    longest = shape.index(max(shape))
    place[longest] = (place[longest] + 1) % shape[longest]
    return drawn.at[tuple(place)].set(high)


def block_scale(own_key, shape, shards, smallest, top_value):
    gain, own = 1.0, jax.random.fold_in(own_key, 6)
    for position, shards_of in shards:
        draws = jnp.exp(jax.random.uniform(jax.random.fold_in(own, position), (shards_of,), jnp.float32, smallest / len(shards), top_value / len(shards)))
        gain = gain * jnp.repeat(draws, shape[position] // shards_of).reshape([-1 if axis == position else 1 for axis in range(len(shape))])
    return gain


def noise(stream_key, dims, deviation, bound, shards=(), kind=jnp.bfloat16):
    entries = deviation * jax.random.normal(stream_key, dims, jnp.float32)
    if shards:
        entries = entries * block_scale(stream_key, dims, shards, -0.22, 0.18)
    return jnp.clip(entries, -bound, bound).astype(kind)


def setup_inputs(seed: int = 0) -> dict:
    key_list = jax.random.split(jax.random.key(seed), 7)
    return {
        "coef": noise(key_list[0], (LEAVES, NC), 1.0, 6.0, ((0, 128),)),
        "tables": noise(key_list[1], (CLASSES, NC, NC), (KNEAR * NC) ** -0.5, 0.09375),
        "leaf_level": touch_ends(jax.random.randint(key_list[2], (LEAVES,), 0, 3), jax.random.fold_in(key_list[2], 1), 0, 2).astype(jnp.int32),
        "inner_list": draw_inner_list(jax.random.fold_in(key_list[6], 71), 0),
        "inner_class": draw_inner_class(jax.random.fold_in(key_list[6], 71), 0),
        "cross_pairs": draw_cross_pairs(jax.random.fold_in(key_list[6], 71), 0),
    }


def spread(rows, classes_of):
    onehot = (classes_of[..., None] == jnp.arange(CLASSES, dtype=jnp.int32)).astype(jnp.float32)
    return jnp.einsum('pkc,pkn->pcn', onehot, rows.astype(jnp.float32)).astype(jnp.bfloat16)


def reference(coef, tables, leaf_level, inner_list, inner_class, cross_pairs):
    table_flat = tables.reshape(CLASSES * NC, NC)
    table_back = jnp.transpose(tables, (0, 2, 1)).reshape(CLASSES * NC, NC)
    bricks = BRICKS_X * BRICKS_Y

    def inner_brick(brick):
        start = (brick * LEAF_DEV).astype(jnp.int32)
        index = lax.dynamic_slice_in_dim(inner_list, start, LEAF_DEV, 0)
        kinds = lax.dynamic_slice_in_dim(inner_class, start, LEAF_DEV, 0)
        slots = spread(coef[index], kinds).reshape(LEAF_DEV, CLASSES * NC)
        return jnp.dot(slots, table_flat, preferred_element_type=jnp.float32)

    near = lax.map(inner_brick, jnp.arange(bricks, dtype=jnp.int32)).reshape(LEAVES, NC)
    blocks = cross_pairs.reshape(3, bricks, CROSS_DEV).transpose(1, 0, 2)

    def cross_brick(block):
        target, source, kinds = block[0], block[1], block[2]
        fwd = jnp.dot(spread(coef[source][:, None, :], kinds[:, None]).reshape(CROSS_DEV, CLASSES * NC), table_flat, preferred_element_type=jnp.float32)
        back = jnp.dot(spread(coef[target][:, None, :], kinds[:, None]).reshape(CROSS_DEV, CLASSES * NC), table_back, preferred_element_type=jnp.float32)
        return fwd, back

    forward, mirror = lax.map(cross_brick, blocks)
    near = near.at[cross_pairs[0]].add(forward.reshape(PAIRS, NC))
    near = near.at[cross_pairs[1]].add(mirror.reshape(PAIRS, NC))
    scale = jnp.power(jnp.float32(0.25), leaf_level.astype(jnp.float32))
    return near * scale[:, None]
```

```python
import jax
import jax.numpy as jnp
from jax import lax
from jax.experimental import pallas as pl
from jax.experimental.pallas import tpu as pltpu
from jax.sharding import PartitionSpec as P


def from_behind(block, axis, distance):
    devices = range(lax.axis_size(axis))
    route = [(i - distance, i) for i in devices if i - distance in devices]
    return lax.ppermute(block, axis, route)


def padded(block, sides, width):
    for axis, dim in sides:
        count = lax.axis_size(axis)
        forward = [(i, i + 1) for i in range(count - 1)]
        backward = [(target, source) for source, target in forward]
        low = lax.ppermute(
            lax.slice_in_dim(block, block.shape[dim] - width, None, axis=dim), axis, forward
        )
        high = lax.ppermute(lax.slice_in_dim(block, 0, width, axis=dim), axis, backward)
        block = jnp.concatenate([low, block, high], axis=dim)
    return block


def classed(rows, kind_ids, flat_tables, classes):
    onehot = (kind_ids[:, None] == jnp.arange(classes, dtype=jnp.int32)[None, :]).astype(rows.dtype)
    slots = (onehot[:, :, None] * rows[:, None, :]).reshape(rows.shape[0], classes * rows.shape[1])
    return jnp.dot(slots, flat_tables, preferred_element_type=jnp.float32)


def pick_rows(index, count, source_rows):
    picker = (index[:, None] == jnp.arange(count, dtype=jnp.int32)[None, :]).astype(
        source_rows.dtype
    )
    return jnp.dot(picker, source_rows, preferred_element_type=jnp.float32).astype(
        source_rows.dtype
    )


def add_rows(index, count, values, valid):
    picker = (
        (index[:, None] == jnp.arange(count, dtype=jnp.int32)[None, :]) & valid[:, None]
    ).astype(jnp.float32)
    return jnp.einsum(
        "pb,pw->bw",
        picker,
        values,
        precision=lax.Precision.HIGHEST,
        preferred_element_type=jnp.float32,
    )


def inner_kernel(coef, tab, idx, out, y, acc):
    c = pl.program_id(0)
    leaf_dev = coef.shape[0]
    rows = 4
    base = c * (rows * leaf_dev)
    half = leaf_dev // 2
    for m in range(0, leaf_dev, half):
        r = jnp.dot(coef[m : m + half, :], tab[0], preferred_element_type=jnp.float32)
        for j in range(rows):
            y[pl.ds(base + rows * m + j, half, stride=rows), :] = r[:, 128 * j : 128 * j + 128]

    @pl.when(c == pl.num_programs(0) - 1)
    def _():
        unroll = 8

        def step(i, _):
            first = (i // 16) * 1024 + (i % 16) * unroll
            for u in range(unroll):
                total = None
                for k in range(8):
                    r = pl.multiple_of(idx[first + (k * 128 + u)], rows)
                    v = y[pl.ds(r, rows), :]
                    total = v if total is None else total + v
                acc[pl.ds(pl.multiple_of(i * (unroll * rows) + u * rows, rows), rows), :] = total
            return 0

        lax.fori_loop(0, leaf_dev // unroll, step, 0)
        for j in range(rows):
            out[:, 128 * j : 128 * j + 128] = acc[pl.ds(j, leaf_dev, stride=rows), :]


def inner_near(coef, tables, local, kinds):
    leaf_dev, width = coef.shape
    classes = tables.shape[0]
    knear = local.shape[1]
    rows = (kinds * leaf_dev + local).T * 4
    rows = rows.reshape(knear, leaf_dev // 128, 128).transpose(1, 0, 2).reshape(-1)
    return pl.pallas_call(
        inner_kernel,
        out_shape=jax.ShapeDtypeStruct((leaf_dev, width), jnp.float32),
        grid=(classes,),
        in_specs=[
            pl.BlockSpec((leaf_dev, width), lambda c: (0, 0)),
            pl.BlockSpec((1, width, width), lambda c: (c, 0, 0)),
            pl.BlockSpec(memory_space=pltpu.SMEM),
        ],
        out_specs=pl.BlockSpec((leaf_dev, width), lambda c: (0, 0)),
        scratch_shapes=[
            pltpu.VMEM((classes * leaf_dev * 4, 128), jnp.float32),
            pltpu.VMEM((leaf_dev * 4, 128), jnp.float32),
        ],
        compiler_params=pltpu.CompilerParams(vmem_limit_bytes=50 << 20),
        cost_estimate=pl.CostEstimate(
            flops=2 * leaf_dev * classes * width * width, bytes_accessed=12 << 20, transcendentals=0
        ),
    )(coef, tables, rows)


def send_direct(piece, offset):
    return from_behind(piece, ("gx", "gy"), offset)


def body(coef, tables, leaf_level, inner_list, inner_class, cross_pairs):
    leaf_dev, width = coef.shape
    classes = tables.shape[0]
    border = leaf_dev // 8
    count_y = lax.axis_size("gy")
    index_x = lax.axis_index("gx")
    index_y = lax.axis_index("gy")
    rank = index_x * count_y + index_y
    offset = rank * leaf_dev
    table_flat = tables.reshape(classes * width, width)
    table_back = jnp.transpose(tables, (0, 2, 1)).reshape(classes * width, width)
    halo_rows = padded(coef[:border][None, None], (("gx", 0), ("gy", 1)), 1)
    halo_rows = halo_rows.reshape(9 * border, width)
    local = inner_list - offset
    near = inner_near(coef, tables, local, inner_class)
    target = cross_pairs[0] - offset
    source = cross_pairs[1]
    kind_ids = cross_pairs[2]
    all_valid = jnp.ones(target.shape, jnp.bool_)
    source_rank = source // leaf_dev
    place_x = source_rank // count_y - index_x + 1
    place_y = source_rank % count_y - index_y + 1
    place = (place_x * 3 + place_y) * border + source % leaf_dev
    source_rows = pick_rows(place, 9 * border, halo_rows)
    forward = classed(source_rows, kind_ids, table_flat, classes)
    border_sum = add_rows(target, border, forward, all_valid)
    target_rows = pick_rows(target, border, coef[:border])
    mirror = classed(target_rows, kind_ids, table_back, classes)
    outgoing = add_rows(place, 9 * border, mirror, all_valid).reshape(3, 3, border, width)
    returned = outgoing[1, 1]
    for step_x in range(3):
        for step_y in range(3):
            if step_x != 1 or step_y != 1:
                returned = returned + send_direct(
                    outgoing[step_x, step_y], (step_x - 1) * count_y + (step_y - 1)
                )
    border_sum = border_sum + returned
    near = near.at[:border].add(border_sum)
    scale = jnp.power(jnp.float32(0.25), leaf_level.astype(jnp.float32))
    return near * scale[:, None]


def solution(mesh):
    return jax.shard_map(
        body,
        mesh=mesh,
        in_specs=(
            P(("gx", "gy"), None),
            P(),
            P(("gx", "gy")),
            P(("gx", "gy"), None),
            P(("gx", "gy"), None),
            P(None, ("gx", "gy")),
        ),
        out_specs=P(("gx", "gy"), None),
        check_vma=False,
    )
```

```python
import functools

import jax
import jax.numpy as jnp
from jax import lax
from jax.experimental import pallas as pl
from jax.experimental.pallas import tpu as pltpu
from jax.sharding import PartitionSpec as P

MESH = pl.DeviceIdType.MESH
ROWS = 4
ROOM = 64
STEPS = [(dx, dy) for dx in (-1, 0, 1) for dy in (-1, 0, 1) if (dx, dy) != (0, 0)]


def dot(a, b):
    return jnp.dot(a, b, preferred_element_type=jnp.float32)


def dot_t(a, b):
    return lax.dot_general(a, b, (((1,), (1,)), ((), ())), preferred_element_type=jnp.float32)


def split(z):
    high = z.astype(jnp.bfloat16)
    return high, (z - high.astype(jnp.float32)).astype(jnp.bfloat16)


def one_hot(mask):
    return jnp.where(mask, 1.0, 0.0).astype(jnp.bfloat16)


def iota(shape, dim):
    return lax.broadcasted_iota(jnp.int32, shape, dim)


def near_kernel(
    size_x,
    size_y,
    coef,
    pairs,
    idx,
    tabs_hbm,
    out,
    border_out,
    most_out,
    halo_out,
    lists_out,
    tabs,
    y,
    acc,
    halo,
    lists,
    g,
    back,
    x_m,
    x_f,
    z_m,
    z_f,
    tab_sem,
    send_sem,
    recv_sem,
    save_sem,
):
    leaf_dev, width = coef.shape
    classes = tabs.shape[0]
    border = leaf_dev // 8
    own = pairs.shape[1]
    my_x, my_y = lax.axis_index("gx"), lax.axis_index("gy")

    def table_copy(c):
        return pltpu.make_async_copy(tabs_hbm.at[c], tabs.at[c], tab_sem.at[c])

    for c in range(classes):
        table_copy(c).start()

    def neighbour(dx, dy):
        return lax.rem(my_x + dx + size_x, size_x), lax.rem(my_y + dy + size_y, size_y)

    barrier = pltpu.get_barrier_semaphore()
    for dx, dy in STEPS:
        pl.semaphore_signal(barrier, inc=1, device_id=neighbour(dx, dy), device_id_type=MESH)
    pl.semaphore_wait(barrier, len(STEPS))
    copies = []
    for there, (dx, dy) in enumerate(STEPS):
        here = len(STEPS) - 1 - there
        for part, (source, target) in enumerate(
            ((pairs, lists.at[here]), (coef.at[pl.ds(0, border)], halo.at[pl.ds(here * border, border)]))
        ):
            copy = pltpu.make_async_remote_copy(
                src_ref=source,
                dst_ref=target,
                send_sem=send_sem.at[part, there],
                recv_sem=recv_sem.at[part, here],
                device_id=neighbour(dx, dy),
                device_id_type=MESH,
            )
            copy.start()
            copies.append(copy)

    def tables_step(i, _):
        for u in range(2):
            c = i * 2 + u
            table_copy(c).wait()
            half = leaf_dev // 2
            for m in range(0, leaf_dev, half):
                r = dot(coef[m : m + half, :], tabs[c])
                for j in range(ROWS):
                    y[pl.ds(c * (ROWS * leaf_dev) + (ROWS * m + j), half, stride=ROWS), :] = r[
                        :, 128 * j : 128 * j + 128
                    ]
        return 0

    lax.fori_loop(0, classes // 2, tables_step, 0)

    for copy in copies:
        copy.wait()
    saves = [
        pltpu.make_async_copy(halo, halo_out, save_sem.at[0]),
        pltpu.make_async_copy(lists, lists_out, save_sem.at[1]),
    ]
    for save in saves:
        save.start()

    target, source, kind = pairs[0:1, :], pairs[1:2, :], pairs[2:3, :]
    rank = my_x * size_y + my_y
    home = source // leaf_dev
    place = (home // size_y - my_x + 1) * 3 + (home % size_y - my_y + 1)
    place = jnp.where(place > 4, place - 1, place)
    row = place * border + source % leaf_dev
    line = iota((128, own), 0)
    columns = jnp.transpose(jnp.where(line == 0, row, kind).astype(jnp.float32))
    row_col = columns[:, 0:1].astype(jnp.int32)
    kind_col = columns[:, 1:2].astype(jnp.int32)
    picker = one_hot(iota((own, halo.shape[0]), 1) == row_col)
    x_f[...] = dot(picker, halo[...]).astype(jnp.bfloat16)

    slots = classes * ROOM
    earlier = one_hot(iota((own, own), 0) < iota((own, own), 1))
    back[...] = jnp.zeros_like(back)

    def list_step(o, carry):
        before, most = carry
        nine = jnp.where(o >= 4, o + 1, o)
        there_x = lax.rem(my_x + nine // 3 - 1 + size_x, size_x)
        there_y = lax.rem(my_y + nine % 3 - 1 + size_y, size_y)
        from_leaf = lists[o, 0:1, :] - (there_x * size_y + there_y) * leaf_dev
        to_leaf = lists[o, 1:2, :] - rank * leaf_dev
        o_kind = lists[o, 2:3, :]
        here = (to_leaf >= 0) & (to_leaf < border)
        kinds = one_hot((iota((classes, own), 0) == o_kind) & here)
        ahead = dot(kinds, earlier) + before
        hits = kinds.astype(jnp.float32)
        place_in = jnp.sum(ahead * hits, axis=0, keepdims=True).astype(jnp.int32)
        most = jnp.maximum(most, jnp.where(here, place_in, 0))
        slot = jnp.where(here & (place_in < ROOM), o_kind * ROOM + place_in, -1)
        e = one_hot(iota((slots, own), 0) == slot)
        lines = iota((2 * border, own), 0)
        w = one_hot(lines == jnp.where(lines < border, from_leaf, to_leaf + border))
        both = dot_t(e, w)
        g[:, pl.ds(pl.multiple_of(o * border, border), border)] = both[:, :border].astype(jnp.bfloat16)
        back[...] += both[:, border:]
        return before + jnp.sum(hits, axis=1, keepdims=True), most

    _, most = lax.fori_loop(
        0,
        len(STEPS),
        list_step,
        (jnp.zeros((classes, 1), jnp.float32), jnp.zeros((1, own), jnp.int32)),
    )
    most_out[...] = jnp.broadcast_to(most, most_out.shape)
    x_m[...] = dot(g[...], halo[...]).astype(jnp.bfloat16)
    z_f[...] = jnp.zeros_like(z_f)

    share = leaf_dev // classes

    def class_step(c, _):
        table = tabs[c]
        rows = jnp.where(kind_col == c, x_f[...].astype(jnp.float32), 0.0).astype(jnp.bfloat16)
        z_f[...] += dot(rows, table)
        at = pl.ds(pl.multiple_of(c * ROOM, ROOM), ROOM)
        z_m[at, :] = dot_t(x_m[at, :], table)
        first = (c // 2) * 1024 + (c % 2) * share
        for u in range(share):
            total = None
            for k in range(8):
                r = idx[first + (k * 128 + u)]
                v = y[pl.ds(r, ROWS), :]
                total = v if total is None else total + v
            acc[pl.ds(pl.multiple_of(c * (share * ROWS) + u * ROWS, ROWS), ROWS), :] = total
        return 0

    lax.fori_loop(0, classes, class_step, 0)

    to_target = one_hot(iota((border, own), 0) == target - rank * leaf_dev)
    to_source = jnp.transpose(back[...]).astype(jnp.bfloat16)
    border_sum = None
    for picks, z in ((to_target, z_f[...]), (to_source, z_m[...])):
        for part in split(z):
            term = dot(picks, part)
            border_sum = term if border_sum is None else border_sum + term
    border_out[...] = border_sum
    for j in range(ROWS):
        out[:, 128 * j : 128 * j + 128] = acc[pl.ds(j, leaf_dev, stride=ROWS), :]
    for save in saves:
        save.wait()


def near_parts(size_x, size_y, coef, tables, pairs, rows):
    leaf_dev, width = coef.shape
    classes = tables.shape[0]
    border = leaf_dev // 8
    own = pairs.shape[1]
    places = len(STEPS)
    slots = classes * ROOM
    vmem = pl.BlockSpec(memory_space=pltpu.VMEM)
    hbm = pl.BlockSpec(memory_space=pl.ANY)
    return pl.pallas_call(
        functools.partial(near_kernel, size_x, size_y),
        out_shape=(
            jax.ShapeDtypeStruct((leaf_dev, width), jnp.float32),
            jax.ShapeDtypeStruct((border, width), jnp.float32),
            jax.ShapeDtypeStruct((8, own), jnp.int32),
            jax.ShapeDtypeStruct((places * border, width), jnp.bfloat16),
            jax.ShapeDtypeStruct((places, *pairs.shape), jnp.int32),
        ),
        in_specs=[vmem, vmem, pl.BlockSpec(memory_space=pltpu.SMEM), hbm],
        out_specs=(vmem, vmem, vmem, hbm, hbm),
        scratch_shapes=[
            pltpu.VMEM((classes, width, width), jnp.bfloat16),
            pltpu.VMEM((classes * leaf_dev * ROWS, 128), jnp.float32),
            pltpu.VMEM((leaf_dev * ROWS, 128), jnp.float32),
            pltpu.VMEM((places * border, width), jnp.bfloat16),
            pltpu.VMEM((places, *pairs.shape), jnp.int32),
            pltpu.VMEM((slots, places * border), jnp.bfloat16),
            pltpu.VMEM((slots, border), jnp.float32),
            pltpu.VMEM((slots, width), jnp.bfloat16),
            pltpu.VMEM((own, width), jnp.bfloat16),
            pltpu.VMEM((slots, width), jnp.float32),
            pltpu.VMEM((own, width), jnp.float32),
            pltpu.SemaphoreType.DMA((classes,)),
            pltpu.SemaphoreType.DMA((2, places)),
            pltpu.SemaphoreType.DMA((2, places)),
            pltpu.SemaphoreType.DMA((2,)),
        ],
        compiler_params=pltpu.CompilerParams(
            collective_id=0, has_side_effects=True, vmem_limit_bytes=60 << 20
        ),
    )(coef, pairs, rows, tables)


def add_rows(index, count, values, valid):
    picker = (
        (index[:, None] == jnp.arange(count, dtype=jnp.int32)[None, :]) & valid[:, None]
    ).astype(jnp.float32)
    return jnp.einsum(
        "pb,pw->bw",
        picker,
        values,
        precision=lax.Precision.HIGHEST,
        preferred_element_type=jnp.float32,
    )


def general_border(size_x, size_y, leaf_dev, halo, lists, pairs, tables):
    classes, width, _ = tables.shape
    border = leaf_dev // 8
    index_x, index_y = lax.axis_index("gx"), lax.axis_index("gy")
    rank = index_x * size_y + index_y
    home = pairs[1] // leaf_dev
    place = (home // size_y - index_x + 1) * 3 + (home % size_y - index_y + 1)
    place = jnp.where(place > 4, place - 1, place)
    picked = jnp.take(halo, place * border + pairs[1] % leaf_dev, axis=0)

    def products(rows, kinds, contract):
        def one(c, total):
            here = jnp.where((kinds == c)[:, None], rows, jnp.zeros_like(rows))
            return total + lax.dot_general(
                here, tables[c], (((1,), (contract,)), ((), ())), preferred_element_type=jnp.float32
            )

        return lax.fori_loop(0, classes, one, jnp.zeros((rows.shape[0], width), jnp.float32))

    everywhere = jnp.ones(pairs[0].shape, jnp.bool_)
    total = add_rows(pairs[0] - rank * leaf_dev, border, products(picked, pairs[2], 0), everywhere)

    def one_place(o, total):
        nine = jnp.where(o >= 4, o + 1, o)
        there_x = lax.rem(index_x + nine // 3 - 1 + size_x, size_x)
        there_y = lax.rem(index_y + nine % 3 - 1 + size_y, size_y)
        there = (there_x * size_y + there_y) * leaf_dev
        here = lists[o, 1] - rank * leaf_dev
        valid = (here >= 0) & (here < border)
        rows = jnp.take(halo, o * border + jnp.clip(lists[o, 0] - there, 0, border - 1), axis=0)
        return total + add_rows(here, border, products(rows, lists[o, 2], 1), valid)

    return lax.fori_loop(0, len(STEPS), one_place, total)


def body(coef, tables, leaf_level, inner_list, inner_class, cross_pairs):
    leaf_dev, width = coef.shape
    knear = inner_list.shape[1]
    border = leaf_dev // 8
    size_x, size_y = lax.axis_size("gx"), lax.axis_size("gy")
    rank = lax.axis_index("gx") * size_y + lax.axis_index("gy")
    rows = (inner_class * leaf_dev + (inner_list - rank * leaf_dev)).T * ROWS
    rows = rows.reshape(knear, leaf_dev // 128, 128).transpose(1, 0, 2).reshape(-1)
    near, border_sum, most, halo, lists = near_parts(
        size_x, size_y, coef, tables, cross_pairs, rows
    )
    border_sum = lax.cond(
        jnp.max(most) >= ROOM,
        lambda: general_border(size_x, size_y, leaf_dev, halo, lists, cross_pairs, tables),
        lambda: border_sum,
    )
    near = near.at[:border].add(border_sum)
    scale = jnp.power(jnp.float32(0.25), leaf_level.astype(jnp.float32))
    return near * scale[:, None]


def solution(mesh):
    return jax.shard_map(
        body,
        mesh=mesh,
        in_specs=(
            P(("gx", "gy"), None),
            P(),
            P(("gx", "gy")),
            P(("gx", "gy"), None),
            P(("gx", "gy"), None),
            P(None, ("gx", "gy")),
        ),
        out_specs=P(("gx", "gy"), None),
        check_vma=False,
    )
```

```python
import functools

import jax
import jax.numpy as jnp
from jax import lax
from jax.experimental import pallas as pl
from jax.experimental.pallas import tpu as pltpu
from jax.sharding import PartitionSpec as P

MESH = pl.DeviceIdType.MESH
ROWS = 4
ROOM = 64
FIRST = 10
STEPS = [(dx, dy) for dx in (-1, 0, 1) for dy in (-1, 0, 1) if (dx, dy) != (0, 0)]


def dot(a, b):
    return jnp.dot(a, b, preferred_element_type=jnp.float32)


def dot_t(a, b):
    return lax.dot_general(a, b, (((1,), (1,)), ((), ())), preferred_element_type=jnp.float32)


def split(z):
    high = z.astype(jnp.bfloat16)
    return high, (z - high.astype(jnp.float32)).astype(jnp.bfloat16)


def one_hot(mask):
    return jnp.where(mask, 1.0, 0.0).astype(jnp.bfloat16)


def iota(shape, dim):
    return lax.broadcasted_iota(jnp.int32, shape, dim)


def near_kernel(
    size_x,
    size_y,
    coef,
    pairs,
    level,
    idx,
    tabs_hbm,
    out_hbm,
    inner_out,
    most_out,
    halo_out,
    lists_out,
    tabs,
    y,
    acc,
    out,
    halo,
    lists,
    g,
    back,
    x_m,
    x_f,
    z_m,
    z_f,
    tab_sem,
    send_sem,
    recv_sem,
    save_sem,
    out_sem,
):
    leaf_dev, width = coef.shape
    classes = tabs.shape[0]
    border = leaf_dev // 8
    own = pairs.shape[1]
    my_x, my_y = lax.axis_index("gx"), lax.axis_index("gy")

    def table_copy(c):
        return pltpu.make_async_copy(tabs_hbm.at[c], tabs.at[c], tab_sem.at[c])

    for c in range(classes):
        table_copy(c).start()

    def neighbour(dx, dy):
        return lax.rem(my_x + dx + size_x, size_x), lax.rem(my_y + dy + size_y, size_y)

    barrier = pltpu.get_barrier_semaphore()
    for dx, dy in STEPS:
        pl.semaphore_signal(barrier, inc=1, device_id=neighbour(dx, dy), device_id_type=MESH)
    def tables_step(i, _):
        for u in range(2):
            c = i * 2 + u
            table_copy(c).wait()
            half = leaf_dev // 2
            for m in range(0, leaf_dev, half):
                r = dot(coef[m : m + half, :], tabs[c])
                for j in range(ROWS):
                    y[pl.ds(c * (ROWS * leaf_dev) + (ROWS * m + j), half, stride=ROWS), :] = r[
                        :, 128 * j : 128 * j + 128
                    ]
        return 0

    lax.fori_loop(0, FIRST // 2, tables_step, 0)
    pl.semaphore_wait(barrier, len(STEPS))
    copies = []
    for there, (dx, dy) in enumerate(STEPS):
        here = len(STEPS) - 1 - there
        for part, (source, target) in enumerate(
            ((pairs, lists.at[here]), (coef.at[pl.ds(0, border)], halo.at[pl.ds(here * border, border)]))
        ):
            copy = pltpu.make_async_remote_copy(
                src_ref=source,
                dst_ref=target,
                send_sem=send_sem.at[part, there],
                recv_sem=recv_sem.at[part, here],
                device_id=neighbour(dx, dy),
                device_id_type=MESH,
            )
            copy.start()
            copies.append(copy)

    lax.fori_loop(FIRST // 2, classes // 2, tables_step, 0)

    unroll = 8

    def leaf_step(i, _):
        first = (i // 16) * 1024 + (i % 16) * unroll
        for u in range(unroll):
            total = None
            for k in range(8):
                r = idx[first + (k * 128 + u)]
                v = y[pl.ds(r, ROWS), :]
                total = v if total is None else total + v
            acc[pl.ds(i * (unroll * ROWS) + u * ROWS, ROWS), :] = total
        return 0

    lax.fori_loop(0, leaf_dev // unroll, leaf_step, 0)

    levels = level[...]
    scale = jnp.ones(levels.shape, jnp.float32)
    for bit in range(3):
        scale = scale * jnp.where((levels & (1 << bit)) != 0, 0.25 ** (1 << bit), 1.0)

    def scales(a):
        return jnp.transpose(jnp.broadcast_to(scale[a : a + 1, :], (128, 128)))

    for a in range(leaf_dev // 128):
        by = scales(a)
        for j in range(ROWS):
            rows = acc[pl.ds(a * 128 * ROWS + j, 128, stride=ROWS), :] * by
            out[a * 128 : a * 128 + 128, 128 * j : 128 * j + 128] = rows
    rest_copy = pltpu.make_async_copy(
        out.at[pl.ds(border, leaf_dev - border)],
        out_hbm.at[pl.ds(border, leaf_dev - border)],
        out_sem.at[0],
    )
    rest_copy.start()

    for copy in copies[0::2]:
        copy.wait()
    target, source, kind = pairs[0:1, :], pairs[1:2, :], pairs[2:3, :]
    rank = my_x * size_y + my_y
    home = source // leaf_dev
    place = (home // size_y - my_x + 1) * 3 + (home % size_y - my_y + 1)
    place = jnp.where(place > 4, place - 1, place)
    row = place * border + source % leaf_dev
    line = iota((128, own), 0)
    columns = jnp.transpose(jnp.where(line == 0, row, kind).astype(jnp.float32))
    row_col = columns[:, 0:1].astype(jnp.int32)
    kind_col = columns[:, 1:2].astype(jnp.int32)
    picker = one_hot(iota((own, halo.shape[0]), 1) == row_col)

    slots = classes * ROOM
    earlier = one_hot(iota((own, own), 0) < iota((own, own), 1))
    back[...] = jnp.zeros_like(back)

    def list_step(o, carry):
        before, most = carry
        nine = jnp.where(o >= 4, o + 1, o)
        there_x = lax.rem(my_x + nine // 3 - 1 + size_x, size_x)
        there_y = lax.rem(my_y + nine % 3 - 1 + size_y, size_y)
        from_leaf = lists[o, 0:1, :] - (there_x * size_y + there_y) * leaf_dev
        to_leaf = lists[o, 1:2, :] - rank * leaf_dev
        o_kind = lists[o, 2:3, :]
        here = (to_leaf >= 0) & (to_leaf < border)
        kinds = one_hot((iota((classes, own), 0) == o_kind) & here)
        ahead = dot(kinds, earlier) + before
        hits = kinds.astype(jnp.float32)
        place_in = jnp.sum(ahead * hits, axis=0, keepdims=True).astype(jnp.int32)
        most = jnp.maximum(most, jnp.where(here, place_in, 0))
        slot = jnp.where(here & (place_in < ROOM), o_kind * ROOM + place_in, -1)
        e = one_hot(iota((slots, own), 0) == slot)
        lines = iota((2 * border, own), 0)
        w = one_hot(lines == jnp.where(lines < border, from_leaf, to_leaf + border))
        both = dot_t(e, w)
        g[:, pl.ds(pl.multiple_of(o * border, border), border)] = both[:, :border].astype(jnp.bfloat16)
        back[...] += both[:, border:]
        return before + jnp.sum(hits, axis=1, keepdims=True), most

    _, most = lax.fori_loop(
        0,
        len(STEPS),
        list_step,
        (jnp.zeros((classes, 1), jnp.float32), jnp.zeros((1, own), jnp.int32)),
    )
    most_out[0] = jnp.max(most)
    to_target = one_hot(iota((border, own), 0) == target - rank * leaf_dev)
    to_source = jnp.transpose(back[...]).astype(jnp.bfloat16)
    for copy in copies[1::2]:
        copy.wait()
    saves = [
        pltpu.make_async_copy(halo, halo_out, save_sem.at[0]),
        pltpu.make_async_copy(lists, lists_out, save_sem.at[1]),
    ]
    for save in saves:
        save.start()
    x_f[...] = dot(picker, halo[...]).astype(jnp.bfloat16)
    x_m[...] = dot(g[...], halo[...]).astype(jnp.bfloat16)
    z_f[...] = jnp.zeros_like(z_f)


    def class_step(c, _):
        table = tabs[c]
        rows = jnp.where(kind_col == c, x_f[...].astype(jnp.float32), 0.0).astype(jnp.bfloat16)
        z_f[...] += dot(rows, table)
        at = pl.ds(pl.multiple_of(c * ROOM, ROOM), ROOM)
        z_m[at, :] = dot_t(x_m[at, :], table)
        return 0

    lax.fori_loop(0, classes, class_step, 0)

    border_sum = None
    for picks, z in ((to_target, z_f[...]), (to_source, z_m[...])):
        for part in split(z):
            term = dot(picks, part)
            border_sum = term if border_sum is None else border_sum + term
    inner_out[...] = out[0:border, :]
    by = scales(0)
    for j in range(ROWS):
        lanes = slice(128 * j, 128 * j + 128)
        out[0:border, lanes] = out[0:border, lanes] + border_sum[:, lanes] * by
    border_copy = pltpu.make_async_copy(
        out.at[pl.ds(0, border)], out_hbm.at[pl.ds(0, border)], out_sem.at[1]
    )
    border_copy.start()
    for save in (*saves, rest_copy, border_copy):
        save.wait()


def near_parts(size_x, size_y, coef, tables, pairs, level, rows):
    leaf_dev, width = coef.shape
    classes = tables.shape[0]
    border = leaf_dev // 8
    own = pairs.shape[1]
    places = len(STEPS)
    slots = classes * ROOM
    vmem = pl.BlockSpec(memory_space=pltpu.VMEM)
    hbm = pl.BlockSpec(memory_space=pl.ANY)
    smem = pl.BlockSpec(memory_space=pltpu.SMEM)
    return pl.pallas_call(
        functools.partial(near_kernel, size_x, size_y),
        out_shape=(
            jax.ShapeDtypeStruct((leaf_dev, width), jnp.float32),
            jax.ShapeDtypeStruct((border, width), jnp.float32),
            jax.ShapeDtypeStruct((1,), jnp.int32),
            jax.ShapeDtypeStruct((places * border, width), jnp.bfloat16),
            jax.ShapeDtypeStruct((places, *pairs.shape), jnp.int32),
        ),
        in_specs=[vmem, vmem, vmem, smem, hbm],
        out_specs=(hbm, vmem, smem, hbm, hbm),
        scratch_shapes=[
            pltpu.VMEM((classes, width, width), jnp.bfloat16),
            pltpu.VMEM((classes * leaf_dev * ROWS, 128), jnp.float32),
            pltpu.VMEM((leaf_dev * ROWS, 128), jnp.float32),
            pltpu.VMEM((leaf_dev, width), jnp.float32),
            pltpu.VMEM((places * border, width), jnp.bfloat16),
            pltpu.VMEM((places, *pairs.shape), jnp.int32),
            pltpu.VMEM((slots, places * border), jnp.bfloat16),
            pltpu.VMEM((slots, border), jnp.float32),
            pltpu.VMEM((slots, width), jnp.bfloat16),
            pltpu.VMEM((own, width), jnp.bfloat16),
            pltpu.VMEM((slots, width), jnp.float32),
            pltpu.VMEM((own, width), jnp.float32),
            pltpu.SemaphoreType.DMA((classes,)),
            pltpu.SemaphoreType.DMA((2, places)),
            pltpu.SemaphoreType.DMA((2, places)),
            pltpu.SemaphoreType.DMA((2,)),
            pltpu.SemaphoreType.DMA((2,)),
        ],
        compiler_params=pltpu.CompilerParams(
            collective_id=0, has_side_effects=True, vmem_limit_bytes=60 << 20
        ),
    )(coef, pairs, level, rows, tables)


def add_rows(index, count, values, valid):
    picker = (
        (index[:, None] == jnp.arange(count, dtype=jnp.int32)[None, :]) & valid[:, None]
    ).astype(jnp.float32)
    return jnp.einsum(
        "pb,pw->bw",
        picker,
        values,
        precision=lax.Precision.HIGHEST,
        preferred_element_type=jnp.float32,
    )


def general_border(size_x, size_y, leaf_dev, halo, lists, pairs, tables):
    classes, width, _ = tables.shape
    border = leaf_dev // 8
    index_x, index_y = lax.axis_index("gx"), lax.axis_index("gy")
    rank = index_x * size_y + index_y
    home = pairs[1] // leaf_dev
    place = (home // size_y - index_x + 1) * 3 + (home % size_y - index_y + 1)
    place = jnp.where(place > 4, place - 1, place)
    picked = jnp.take(halo, place * border + pairs[1] % leaf_dev, axis=0)

    def products(rows, kinds, contract):
        def one(c, total):
            here = jnp.where((kinds == c)[:, None], rows, jnp.zeros_like(rows))
            return total + lax.dot_general(
                here, tables[c], (((1,), (contract,)), ((), ())), preferred_element_type=jnp.float32
            )

        return lax.fori_loop(0, classes, one, jnp.zeros((rows.shape[0], width), jnp.float32))

    everywhere = jnp.ones(pairs[0].shape, jnp.bool_)
    total = add_rows(pairs[0] - rank * leaf_dev, border, products(picked, pairs[2], 0), everywhere)

    def one_place(o, total):
        nine = jnp.where(o >= 4, o + 1, o)
        there_x = lax.rem(index_x + nine // 3 - 1 + size_x, size_x)
        there_y = lax.rem(index_y + nine % 3 - 1 + size_y, size_y)
        there = (there_x * size_y + there_y) * leaf_dev
        here = lists[o, 1] - rank * leaf_dev
        valid = (here >= 0) & (here < border)
        rows = jnp.take(halo, o * border + jnp.clip(lists[o, 0] - there, 0, border - 1), axis=0)
        return total + add_rows(here, border, products(rows, lists[o, 2], 1), valid)

    return lax.fori_loop(0, len(STEPS), one_place, total)


def body(coef, tables, leaf_level, inner_list, inner_class, cross_pairs):
    leaf_dev, width = coef.shape
    knear = inner_list.shape[1]
    border = leaf_dev // 8
    size_x, size_y = lax.axis_size("gx"), lax.axis_size("gy")
    rank = lax.axis_index("gx") * size_y + lax.axis_index("gy")
    rows = (inner_class * leaf_dev + (inner_list - rank * leaf_dev)).T * ROWS
    rows = rows.reshape(knear, leaf_dev // 128, 128).transpose(1, 0, 2).reshape(-1)
    level = leaf_level.reshape(leaf_dev // 128, 128)
    out, inner, most, halo, lists = near_parts(
        size_x, size_y, coef, tables, cross_pairs, level, rows
    )

    def general(out):
        border_sum = general_border(size_x, size_y, leaf_dev, halo, lists, cross_pairs, tables)
        scale = jnp.power(jnp.float32(0.25), leaf_level[:border].astype(jnp.float32))
        return out.at[:border].set(inner + border_sum * scale[:, None])

    return lax.cond(most[0] >= ROOM, general, lambda out: out, out)


def solution(mesh):
    return jax.shard_map(
        body,
        mesh=mesh,
        in_specs=(
            P(("gx", "gy"), None),
            P(),
            P(("gx", "gy")),
            P(("gx", "gy"), None),
            P(("gx", "gy"), None),
            P(None, ("gx", "gy")),
        ),
        out_specs=P(("gx", "gy"), None),
        check_vma=False,
    )
```

```python
import functools

import jax
import jax.numpy as jnp
from jax import lax
from jax.experimental import pallas as pl
from jax.experimental.pallas import tpu as pltpu
from jax.sharding import PartitionSpec as P

MESH = pl.DeviceIdType.MESH
ROWS = 4
ROOM = 64
FIRST = 8
SLOTS = 4
STEPS = [(-1, -1), (-1, 0), (-1, 1), (1, -1), (1, 0), (1, 1), (0, -1), (0, 1)]


def place_of(dx, dy):
    if isinstance(dx, int):
        return {-1: dy + 1, 1: dy + 4, 0: 6 + (dy + 1) // 2}[dx]
    return jnp.where(dx < 0, dy + 1, jnp.where(dx > 0, dy + 4, 6 + (dy + 1) // 2))


def dot(a, b):
    return jnp.dot(a, b, preferred_element_type=jnp.float32)


def dot_t(a, b):
    return lax.dot_general(a, b, (((1,), (1,)), ((), ())), preferred_element_type=jnp.float32)


def split(z):
    high = z.astype(jnp.bfloat16)
    return high, (z - high.astype(jnp.float32)).astype(jnp.bfloat16)


def one_hot(mask):
    return jnp.where(mask, 1.0, 0.0).astype(jnp.bfloat16)


def iota(shape, dim):
    return lax.broadcasted_iota(jnp.int32, shape, dim)


def scale_of(levels):
    scale = jnp.ones(levels.shape, jnp.float32)
    for bit in range(3):
        scale = scale * jnp.where((levels & (1 << bit)) != 0, 0.25 ** (1 << bit), 1.0)
    return scale


def down(scale, a):
    return jnp.transpose(jnp.broadcast_to(scale[a : a + 1, :], (128, 128)))


def near_kernel(
    size_x,
    size_y,
    coef,
    pairs,
    level,
    inner_list,
    inner_class,
    tabs_hbm,
    rest_out,
    border_out,
    inner_out,
    most_out,
    halo_out,
    lists_out,
    tabs,
    y,
    acc,
    out,
    idx,
    idx_slot,
    halo,
    lists,
    g,
    back,
    x_m,
    x_f,
    z_m,
    z_f,
    tab_sem,
    send_sem,
    recv_sem,
    save_sem,
    out_sem,
    idx_sem,
):
    leaf_dev, width = coef.shape
    classes = tabs.shape[0]
    border = leaf_dev // 8
    own = pairs.shape[1]
    my_x, my_y = lax.axis_index("gx"), lax.axis_index("gy")

    def table_copy(c):
        return pltpu.make_async_copy(tabs_hbm.at[c], tabs.at[c], tab_sem.at[c])

    for c in range(classes):
        table_copy(c).start()

    def neighbour(dx, dy):
        return lax.rem(my_x + dx + size_x, size_x), lax.rem(my_y + dy + size_y, size_y)

    barrier = pltpu.get_barrier_semaphore()
    for dx, dy in STEPS:
        pl.semaphore_signal(barrier, inc=1, device_id=neighbour(dx, dy), device_id_type=MESH)
    idx[...] = ((inner_class[...] & (classes - 1)) * leaf_dev + (inner_list[...] & (leaf_dev - 1))) * ROWS

    def idx_copy(chunk, slot):
        lanes = pl.ds(pl.multiple_of(chunk * 128, 128), 128)
        return pltpu.make_async_copy(idx.at[:, lanes], idx_slot.at[slot], idx_sem.at[slot])

    def tables_step(i, _):
        for u in range(2):
            c = i * 2 + u
            table_copy(c).wait()
            half = leaf_dev // 2
            for m in range(0, leaf_dev, half):
                r = dot(coef[m : m + half, :], tabs[c])
                for j in range(ROWS):
                    y[pl.ds(c * (ROWS * leaf_dev) + (ROWS * m + j), half, stride=ROWS), :] = r[
                        :, 128 * j : 128 * j + 128
                    ]
        return 0

    lax.fori_loop(0, FIRST // 2, tables_step, 0)
    pl.semaphore_wait(barrier, len(STEPS))
    mate = 1 - 2 * lax.rem(my_y, 2)

    def rows_of(place):
        return halo.at[pl.ds(place * border, border)]

    def halo_copy(source, sent, place, dx, dy):
        return pltpu.make_async_remote_copy(
            src_ref=source,
            dst_ref=rows_of(place),
            send_sem=send_sem.at[0, sent],
            recv_sem=recv_sem.at[0, place],
            device_id=neighbour(dx, dy),
            device_id_type=MESH,
        )

    list_copies = []
    for there, (dx, dy) in enumerate(STEPS):
        copy = pltpu.make_async_remote_copy(
            src_ref=pairs,
            dst_ref=lists.at[place_of(-dx, -dy)],
            send_sem=send_sem.at[1, there],
            recv_sem=recv_sem.at[1, place_of(-dx, -dy)],
            device_id=neighbour(dx, dy),
            device_id_type=MESH,
        )
        copy.start()
        list_copies.append(copy)
    mine = coef.at[pl.ds(0, border)]
    sends = [(0, -mate), (-1, -mate), (1, -mate), (-1, 0), (1, 0), (0, mate)]
    halo_copies = [
        halo_copy(mine, sent, place_of(-dx, -dy), dx, dy) for sent, (dx, dy) in enumerate(sends)
    ]
    for copy in halo_copies:
        copy.start()
    for slot in range(SLOTS):
        idx_copy(slot, slot).start()
    lax.fori_loop(FIRST // 2, classes // 2, tables_step, 0)

    def leaf_step(i, _):
        for slot in range(SLOTS):
            chunk = i * SLOTS + slot
            idx_copy(chunk, slot).wait()
            for u in range(128):
                total = None
                for k in range(8):
                    v = y[pl.ds(idx_slot[slot, k, u], ROWS), :]
                    total = v if total is None else total + v
                acc[pl.ds(chunk * (128 * ROWS) + u * ROWS, ROWS), :] = total

            idx_copy(lax.rem(chunk + SLOTS, leaf_dev // 128), slot).start()
        return 0

    lax.fori_loop(0, leaf_dev // 128 // SLOTS, leaf_step, 0)
    for slot in range(SLOTS):
        idx_copy(slot, slot).wait()

    scale = scale_of(level[...])

    for a in range(leaf_dev // 128):
        by = down(scale, a)
        for j in range(ROWS):
            rows = acc[pl.ds(a * 128 * ROWS + j, 128, stride=ROWS), :] * by
            out[a * 128 : a * 128 + 128, 128 * j : 128 * j + 128] = rows
    rest_copy = pltpu.make_async_copy(
        out.at[pl.ds(border, leaf_dev - border)], rest_out, out_sem.at[0]
    )
    rest_copy.start()

    for sent, dx in ((6, -1), (7, 1)):
        came = place_of(dx, 0)
        halo_copy(rows_of(came), sent, came, 0, mate).wait_recv()
        copy = halo_copy(rows_of(came), sent, place_of(dx, -mate), 0, mate)
        copy.start()
        halo_copies.append(copy)
    for copy in list_copies:
        copy.wait()
    target, source, kind = pairs[0:1, :], pairs[1:2, :], pairs[2:3, :]
    rank = my_x * size_y + my_y
    home = source // leaf_dev
    place = place_of(home // size_y - my_x, home % size_y - my_y)
    row = place * border + source % leaf_dev
    line = iota((128, own), 0)
    columns = jnp.transpose(jnp.where(line == 0, row, kind).astype(jnp.float32))
    row_col = columns[:, 0:1].astype(jnp.int32)
    kind_col = columns[:, 1:2].astype(jnp.int32)
    picker = one_hot(iota((own, halo.shape[0]), 1) == row_col)

    slots = classes * ROOM
    earlier = one_hot(iota((own, own), 0) < iota((own, own), 1))
    back[...] = jnp.zeros_like(back)

    def list_step(o, carry):
        before, most = carry
        from_leaf = lists[o, 0:1, :] % leaf_dev
        to_leaf = lists[o, 1:2, :] - rank * leaf_dev
        o_kind = lists[o, 2:3, :]
        here = (to_leaf >= 0) & (to_leaf < border)
        kinds = one_hot((iota((classes, own), 0) == o_kind) & here)
        ahead = dot(kinds, earlier) + before
        hits = kinds.astype(jnp.float32)
        place_in = jnp.sum(ahead * hits, axis=0, keepdims=True).astype(jnp.int32)
        most = jnp.maximum(most, jnp.where(here, place_in, 0))
        room = one_hot(iota((ROOM, own), 0) == place_in)
        e = jnp.concatenate([room * kinds[c : c + 1, :] for c in range(classes)], axis=0)
        lines = iota((2 * border, own), 0)
        w = one_hot(lines == jnp.where(lines < border, from_leaf, to_leaf + border))
        both = dot_t(e, w)
        g[:, pl.ds(pl.multiple_of(o * border, border), border)] = both[:, :border].astype(jnp.bfloat16)
        back[...] += both[:, border:]
        return before + jnp.sum(hits, axis=1, keepdims=True), most

    _, most = lax.fori_loop(
        0,
        len(STEPS),
        list_step,
        (jnp.zeros((classes, 1), jnp.float32), jnp.zeros((1, own), jnp.int32)),
    )
    most_out[0] = jnp.max(most)
    to_target = one_hot(iota((border, own), 0) == target - rank * leaf_dev)
    to_source = jnp.transpose(back[...]).astype(jnp.bfloat16)
    for copy in halo_copies:
        copy.wait_send()
    for place in range(len(STEPS)):
        if place not in (place_of(-1, 0), place_of(1, 0)):
            halo_copy(rows_of(place), 0, place, 0, mate).wait_recv()
    saves = [
        pltpu.make_async_copy(halo, halo_out.at[pl.ds(0, halo.shape[0])], save_sem.at[0]),
        pltpu.make_async_copy(lists, lists_out, save_sem.at[1]),
    ]
    for save in saves:
        save.start()
    x_f[...] = dot(picker, halo[...]).astype(jnp.bfloat16)
    x_m[...] = dot(g[...], halo[...]).astype(jnp.bfloat16)


    for c in range(classes):
        rows = jnp.where(kind_col == c, x_f[...].astype(jnp.float32), 0.0).astype(jnp.bfloat16)
        part = dot(rows, tabs[c])
        z_f[...] = part if c == 0 else z_f[...] + part
        z_m[c * ROOM : (c + 1) * ROOM, :] = dot_t(x_m[c * ROOM : (c + 1) * ROOM, :], tabs[c])

    border_sum = None
    for picks, z in ((to_target, z_f[...]), (to_source, z_m[...])):
        for part in split(z):
            term = dot(picks, part)
            border_sum = term if border_sum is None else border_sum + term
    inner_out[...] = out[0:border, :]
    by = down(scale, 0)
    for j in range(ROWS):
        lanes = slice(128 * j, 128 * j + 128)
        border_out[:, lanes] = out[0:border, lanes] + border_sum[:, lanes] * by
    for save in (*saves, rest_copy):
        save.wait()


def near_parts(size_x, size_y, coef, tables, pairs, level, inner_list, inner_class):
    leaf_dev, width = coef.shape
    classes = tables.shape[0]
    border = leaf_dev // 8
    own = pairs.shape[1]
    places = len(STEPS)
    slots = classes * ROOM
    vmem = pl.BlockSpec(memory_space=pltpu.VMEM)
    hbm = pl.BlockSpec(memory_space=pl.ANY)
    smem = pl.BlockSpec(memory_space=pltpu.SMEM)
    return pl.pallas_call(
        functools.partial(near_kernel, size_x, size_y),
        out_shape=(
            jax.ShapeDtypeStruct((leaf_dev - border, width), jnp.float32),
            jax.ShapeDtypeStruct((border, width), jnp.float32),
            jax.ShapeDtypeStruct((border, width), jnp.float32),
            jax.ShapeDtypeStruct((1,), jnp.int32),
            jax.ShapeDtypeStruct((12 * places * border, width), jnp.bfloat16),
            jax.ShapeDtypeStruct((places, *pairs.shape), jnp.int32),
        ),
        in_specs=[vmem, vmem, vmem, vmem, vmem, hbm],
        out_specs=(hbm, vmem, vmem, smem, hbm, hbm),
        scratch_shapes=[
            pltpu.VMEM((classes, width, width), jnp.bfloat16),
            pltpu.VMEM((classes * leaf_dev * ROWS, 128), jnp.float32),
            pltpu.VMEM((leaf_dev * ROWS, 128), jnp.float32),
            pltpu.VMEM((leaf_dev, width), jnp.float32),
            pltpu.VMEM(inner_list.shape, jnp.int32),
            pltpu.SMEM((SLOTS, inner_list.shape[0], 128), jnp.int32),
            pltpu.VMEM((places * border, width), jnp.bfloat16),
            pltpu.VMEM((places, *pairs.shape), jnp.int32),
            pltpu.VMEM((slots, places * border), jnp.bfloat16),
            pltpu.VMEM((slots, border), jnp.float32),
            pltpu.VMEM((slots, width), jnp.bfloat16),
            pltpu.VMEM((own, width), jnp.bfloat16),
            pltpu.VMEM((slots, width), jnp.float32),
            pltpu.VMEM((own, width), jnp.float32),
            pltpu.SemaphoreType.DMA((classes,)),
            pltpu.SemaphoreType.DMA((2, places)),
            pltpu.SemaphoreType.DMA((2, places)),
            pltpu.SemaphoreType.DMA((2,)),
            pltpu.SemaphoreType.DMA((1,)),
            pltpu.SemaphoreType.DMA((SLOTS,)),
        ],
        compiler_params=pltpu.CompilerParams(
            collective_id=0, has_side_effects=True, vmem_limit_bytes=54 << 20
        ),
    )(coef, pairs, level, inner_list, inner_class, tables)


def finish_kernel(
    size_x,
    size_y,
    most,
    rest,
    fast,
    inner,
    halo_hbm,
    lists_hbm,
    pairs_hbm,
    level_hbm,
    tabs_hbm,
    out,
    halo,
    lists,
    pairs,
    level,
    table,
    total,
    final,
    whole,
    sem,
):
    border, width = total.shape
    own = pairs.shape[1]
    leaf_dev = out.shape[0]
    pieces = leaf_dev // border

    def piece(i):
        return pl.ds(i * border, border)

    taken = [
        pltpu.make_async_copy(rest.at[piece(i - 1)] if i else fast, whole.at[piece(i)], sem.at[0, i])
        for i in range(pieces)
    ]
    given = [pltpu.make_async_copy(whole.at[piece(i)], out.at[piece(i)], sem.at[1, i]) for i in range(pieces)]
    for copy in taken:
        copy.start()
    for copy, onward in zip(taken, given, strict=True):
        copy.wait()
        onward.start()
    for copy in given:
        copy.wait()

    @pl.when(most[0] >= ROOM)
    def _():
        def bring(source, target):
            copy = pltpu.make_async_copy(source, target, sem.at[0, 0])
            copy.start()
            copy.wait()

        bring(halo_hbm.at[pl.ds(0, halo.shape[0])], halo)
        bring(lists_hbm, lists)
        bring(pairs_hbm, pairs)
        bring(level_hbm, level)
        my_x, my_y = lax.axis_index("gx"), lax.axis_index("gy")
        rank = my_x * size_y + my_y

        def add(row, kind, at, times):
            line = iota((128, own), 0)
            columns = jnp.transpose(jnp.where(line == 0, row, kind).astype(jnp.float32))
            row_col = columns[:, 0:1].astype(jnp.int32)
            kind_col = columns[:, 1:2].astype(jnp.int32)
            rows = dot(one_hot(iota((own, halo.shape[0]), 1) == row_col), halo[...])
            picks = one_hot(iota((border, own), 0) == at)

            def class_step(c, _):
                bring(tabs_hbm.at[c], table)
                for part in split(times(jnp.where(kind_col == c, rows, 0.0).astype(jnp.bfloat16), table[...])):
                    total[...] += dot(picks, part)
                return 0

            lax.fori_loop(0, tabs_hbm.shape[0], class_step, 0)

        total[...] = jnp.zeros_like(total)
        target, source, kind = pairs[0:1, :], pairs[1:2, :], pairs[2:3, :]
        home = source // leaf_dev
        place = place_of(home // size_y - my_x, home % size_y - my_y)
        add(place * border + source % leaf_dev, kind, target - rank * leaf_dev, dot)

        def list_step(o, _):
            row = o * border + lists[o, 0:1, :] % leaf_dev
            add(row, lists[o, 2:3, :], lists[o, 1:2, :] - rank * leaf_dev, dot_t)
            return 0

        lax.fori_loop(0, lists.shape[0], list_step, 0)
        bring(inner, final)
        by = down(scale_of(level[...]), 0)
        for j in range(width // 128):
            lanes = slice(128 * j, 128 * j + 128)
            final[:, lanes] = final[:, lanes] + total[:, lanes] * by
        bring(final, out.at[pl.ds(0, border)])


def finish(size_x, size_y, most, rest, fast, inner, halo, lists, pairs, level, tables):
    border, width = fast.shape
    hbm = pl.BlockSpec(memory_space=pl.ANY)
    return pl.pallas_call(
        functools.partial(finish_kernel, size_x, size_y),
        out_shape=jax.ShapeDtypeStruct((rest.shape[0] + border, width), jnp.float32),
        in_specs=[pl.BlockSpec(memory_space=pltpu.SMEM)] + [hbm] * 8,
        out_specs=hbm,
        scratch_shapes=[
            pltpu.VMEM((len(STEPS) * border, width), jnp.bfloat16),
            pltpu.VMEM(lists.shape, jnp.int32),
            pltpu.VMEM(pairs.shape, jnp.int32),
            pltpu.VMEM(level.shape, jnp.int32),
            pltpu.VMEM(tables.shape[1:], jnp.bfloat16),
            pltpu.VMEM((border, width), jnp.float32),
            pltpu.VMEM((border, width), jnp.float32),
            pltpu.VMEM((rest.shape[0] + border, width), jnp.float32),
            pltpu.SemaphoreType.DMA((2, rest.shape[0] // border + 1)),
        ],
        compiler_params=pltpu.CompilerParams(vmem_limit_bytes=60 << 20),
    )(most, rest, fast, inner, halo, lists, pairs, level, tables)


def body(coef, tables, leaf_level, inner_list, inner_class, cross_pairs):
    leaf_dev, width = coef.shape
    size_x, size_y = lax.axis_size("gx"), lax.axis_size("gy")
    level = leaf_level.reshape(leaf_dev // 128, 128)
    rest, fast, inner, most, halo, lists = near_parts(
        size_x, size_y, coef, tables, cross_pairs, level, inner_list.T, inner_class.T
    )

    return finish(size_x, size_y, most, rest, fast, inner, halo, lists, cross_pairs, level, tables)


def solution(mesh):
    return jax.shard_map(
        body,
        mesh=mesh,
        in_specs=(
            P(("gx", "gy"), None),
            P(),
            P(("gx", "gy")),
            P(("gx", "gy"), None),
            P(("gx", "gy"), None),
            P(None, ("gx", "gy")),
        ),
        out_specs=P(("gx", "gy"), None),
        check_vma=False,
    )
```

```python
import functools

import jax
import jax.numpy as jnp
from jax import lax
from jax.experimental import pallas as pl
from jax.experimental.pallas import tpu as pltpu
from jax.sharding import PartitionSpec as P

MESH = pl.DeviceIdType.MESH
ROWS = 4
ROOM = 64
FIRST = 6
SLOTS = 4
STEPS = [(-1, -1), (-1, 0), (-1, 1), (1, -1), (1, 0), (1, 1), (0, -1), (0, 1)]


def place_of(dx, dy):
    if isinstance(dx, int):
        return {-1: dy + 1, 1: dy + 4, 0: 6 + (dy + 1) // 2}[dx]
    return jnp.where(dx < 0, dy + 1, jnp.where(dx > 0, dy + 4, 6 + (dy + 1) // 2))


def dot(a, b):
    return jnp.dot(a, b, preferred_element_type=jnp.float32)


def dot_t(a, b):
    return lax.dot_general(a, b, (((1,), (1,)), ((), ())), preferred_element_type=jnp.float32)


def split(z):
    high = z.astype(jnp.bfloat16)
    return high, (z - high.astype(jnp.float32)).astype(jnp.bfloat16)


def one_hot(mask):
    return jnp.where(mask, 1.0, 0.0).astype(jnp.bfloat16)


def iota(shape, dim):
    return lax.broadcasted_iota(jnp.int32, shape, dim)


def scale_of(levels):
    scale = jnp.ones(levels.shape, jnp.float32)
    for bit in range(3):
        scale = scale * jnp.where((levels & (1 << bit)) != 0, 0.25 ** (1 << bit), 1.0)
    return scale


def down(scale, a):
    return jnp.transpose(jnp.broadcast_to(scale[a : a + 1, :], (128, 128)))


def near_kernel(
    size_x,
    size_y,
    coef_hbm,
    pairs_hbm,
    level_hbm,
    inner_list_hbm,
    inner_class_hbm,
    tabs_hbm,
    rest_out,
    border_out,
    inner_out,
    most_out,
    halo_out,
    lists_out,
    coef,
    pairs,
    level,
    inner_list,
    inner_class,
    tabs,
    y,
    acc,
    out,
    idx,
    idx_slot,
    halo,
    lists,
    g,
    back,
    x_m,
    x_f,
    z_m,
    z_f,
    tab_sem,
    send_sem,
    recv_sem,
    save_sem,
    out_sem,
    idx_sem,
    arg_sem,
):
    leaf_dev, width = coef.shape
    classes = tabs.shape[0]
    border = leaf_dev // 8
    own = pairs.shape[1]
    my_x, my_y = lax.axis_index("gx"), lax.axis_index("gy")

    def table_copy(c):
        return pltpu.make_async_copy(tabs_hbm.at[c], tabs.at[c], tab_sem.at[c])

    arguments = [
        pltpu.make_async_copy(source, target, arg_sem.at[i])
        for i, (source, target) in enumerate(
            (
                (coef_hbm, coef),
                (pairs_hbm, pairs),
                (level_hbm, level),
                (inner_list_hbm, inner_list),
                (inner_class_hbm, inner_class),
            )
        )
    ]
    arguments[0].start()
    for c in range(2):
        table_copy(c).start()
    for argument in arguments[1:]:
        argument.start()
    for c in range(2, classes):
        table_copy(c).start()

    def neighbour(dx, dy):
        return lax.rem(my_x + dx + size_x, size_x), lax.rem(my_y + dy + size_y, size_y)

    barrier = pltpu.get_barrier_semaphore()
    for dx, dy in STEPS:
        pl.semaphore_signal(barrier, inc=1, device_id=neighbour(dx, dy), device_id_type=MESH)

    def idx_copy(chunk, slot):
        lanes = pl.ds(pl.multiple_of(chunk * 128, 128), 128)
        return pltpu.make_async_copy(idx.at[:, lanes], idx_slot.at[slot], idx_sem.at[slot])

    def tables_step(i, _):
        for u in range(2):
            c = i * 2 + u
            table_copy(c).wait()
            half = leaf_dev // 2
            for m in range(0, leaf_dev, half):
                r = dot(coef[m : m + half, :], tabs[c])
                for j in range(ROWS):
                    y[pl.ds(c * (ROWS * leaf_dev) + (ROWS * m + j), half, stride=ROWS), :] = r[
                        :, 128 * j : 128 * j + 128
                    ]
        return 0

    arguments[0].wait()
    lax.fori_loop(0, FIRST // 2, tables_step, 0)
    for argument in arguments[1:]:
        argument.wait()
    pl.semaphore_wait(barrier, len(STEPS))
    mate = 1 - 2 * lax.rem(my_y, 2)

    def rows_of(place):
        return halo.at[pl.ds(place * border, border)]

    def halo_copy(source, sent, place, dx, dy):
        return pltpu.make_async_remote_copy(
            src_ref=source,
            dst_ref=rows_of(place),
            send_sem=send_sem.at[0, sent],
            recv_sem=recv_sem.at[0, place],
            device_id=neighbour(dx, dy),
            device_id_type=MESH,
        )

    list_copies = []
    for there, (dx, dy) in enumerate(STEPS):
        copy = pltpu.make_async_remote_copy(
            src_ref=pairs,
            dst_ref=lists.at[place_of(-dx, -dy)],
            send_sem=send_sem.at[1, there],
            recv_sem=recv_sem.at[1, place_of(-dx, -dy)],
            device_id=neighbour(dx, dy),
            device_id_type=MESH,
        )
        copy.start()
        list_copies.append(copy)
    mine = coef.at[pl.ds(0, border)]
    sends = [(-1, 0), (1, 0), (0, -mate), (-1, -mate), (1, -mate), (0, mate)]
    halo_copies = [
        halo_copy(mine, sent, place_of(-dx, -dy), dx, dy) for sent, (dx, dy) in enumerate(sends)
    ]
    for copy in halo_copies:
        copy.start()
    idx[...] = ((inner_class[...] & (classes - 1)) * leaf_dev + (inner_list[...] & (leaf_dev - 1))) * ROWS
    for slot in range(SLOTS):
        idx_copy(slot, slot).start()
    lax.fori_loop(FIRST // 2, classes // 2, tables_step, 0)

    def leaf_step(i, _):
        for slot in range(SLOTS):
            chunk = i * SLOTS + slot
            idx_copy(chunk, slot).wait()
            for u in range(128):
                total = None
                for k in range(8):
                    v = y[pl.ds(idx_slot[slot, k, u], ROWS), :]
                    total = v if total is None else total + v
                acc[pl.ds(chunk * (128 * ROWS) + u * ROWS, ROWS), :] = total

            idx_copy(lax.rem(chunk + SLOTS, leaf_dev // 128), slot).start()
        return 0

    lax.fori_loop(0, leaf_dev // 128 // SLOTS, leaf_step, 0)
    for slot in range(SLOTS):
        idx_copy(slot, slot).wait()

    scale = scale_of(level[...])

    for a in range(leaf_dev // 128):
        by = down(scale, a)
        for j in range(ROWS):
            rows = acc[pl.ds(a * 128 * ROWS + j, 128, stride=ROWS), :] * by
            out[a * 128 : a * 128 + 128, 128 * j : 128 * j + 128] = rows
    rest_copy = pltpu.make_async_copy(
        out.at[pl.ds(border, leaf_dev - border)], rest_out, out_sem.at[0]
    )
    rest_copy.start()

    for sent, dx in ((6, -1), (7, 1)):
        came = place_of(dx, 0)
        halo_copy(rows_of(came), sent, came, 0, mate).wait_recv()
        copy = halo_copy(rows_of(came), sent, place_of(dx, -mate), 0, mate)
        copy.start()
        halo_copies.append(copy)
    for copy in list_copies:
        copy.wait()
    target, source, kind = pairs[0:1, :], pairs[1:2, :], pairs[2:3, :]
    rank = my_x * size_y + my_y
    home = source // leaf_dev
    place = place_of(home // size_y - my_x, home % size_y - my_y)
    row = place * border + source % leaf_dev
    line = iota((128, own), 0)
    columns = jnp.transpose(jnp.where(line == 0, row, kind).astype(jnp.float32))
    row_col = columns[:, 0:1].astype(jnp.int32)
    kind_col = columns[:, 1:2].astype(jnp.int32)
    picker = one_hot(iota((own, halo.shape[0]), 1) == row_col)

    slots = classes * ROOM
    earlier = one_hot(iota((own, own), 0) < iota((own, own), 1))
    back[...] = jnp.zeros_like(back)

    before = jnp.zeros((classes, 1), jnp.float32)
    most = jnp.zeros((1, own), jnp.int32)
    for o in range(len(STEPS)):
        from_leaf = lists[o, 0:1, :] % leaf_dev
        to_leaf = lists[o, 1:2, :] - rank * leaf_dev
        o_kind = lists[o, 2:3, :]
        here = (to_leaf >= 0) & (to_leaf < border)
        kinds = one_hot((iota((classes, own), 0) == o_kind) & here)
        ahead = dot(kinds, earlier) + before
        hits = kinds.astype(jnp.float32)
        place_in = jnp.sum(ahead * hits, axis=0, keepdims=True).astype(jnp.int32)
        most = jnp.maximum(most, jnp.where(here, place_in, 0))
        room = one_hot(iota((ROOM, own), 0) == place_in)
        e = jnp.concatenate([room * kinds[c : c + 1, :] for c in range(classes)], axis=0)
        lines = iota((2 * border, own), 0)
        w = one_hot(lines == jnp.where(lines < border, from_leaf, to_leaf + border))
        both = dot_t(e, w)
        g[:, o * border : (o + 1) * border] = both[:, :border].astype(jnp.bfloat16)
        back[...] += both[:, border:]
        before = before + jnp.sum(hits, axis=1, keepdims=True)
    most_out[0] = jnp.max(most)
    to_target = one_hot(iota((border, own), 0) == target - rank * leaf_dev)
    to_source = jnp.transpose(back[...]).astype(jnp.bfloat16)
    for copy in halo_copies:
        copy.wait_send()
    for place in range(len(STEPS)):
        if place not in (place_of(-1, 0), place_of(1, 0)):
            halo_copy(rows_of(place), 0, place, 0, mate).wait_recv()
    saves = [
        pltpu.make_async_copy(halo, halo_out.at[pl.ds(0, halo.shape[0])], save_sem.at[0]),
        pltpu.make_async_copy(lists, lists_out, save_sem.at[1]),
    ]
    for save in saves:
        save.start()
    x_f[...] = dot(picker, halo[...]).astype(jnp.bfloat16)
    x_m[...] = dot(g[...], halo[...]).astype(jnp.bfloat16)


    for c in range(classes):
        rows = jnp.where(kind_col == c, x_f[...].astype(jnp.float32), 0.0).astype(jnp.bfloat16)
        part = dot(rows, tabs[c])
        z_f[...] = part if c == 0 else z_f[...] + part
        z_m[c * ROOM : (c + 1) * ROOM, :] = dot_t(x_m[c * ROOM : (c + 1) * ROOM, :], tabs[c])

    border_sum = None
    for picks, z in ((to_target, z_f[...]), (to_source, z_m[...])):
        for part in split(z):
            term = dot(picks, part)
            border_sum = term if border_sum is None else border_sum + term
    inner_out[...] = out[0:border, :]
    by = down(scale, 0)
    for j in range(ROWS):
        lanes = slice(128 * j, 128 * j + 128)
        border_out[:, lanes] = out[0:border, lanes] + border_sum[:, lanes] * by
    for save in (*saves, rest_copy):
        save.wait()


def near_parts(size_x, size_y, coef, tables, pairs, level, inner_list, inner_class):
    leaf_dev, width = coef.shape
    classes = tables.shape[0]
    border = leaf_dev // 8
    own = pairs.shape[1]
    places = len(STEPS)
    slots = classes * ROOM
    vmem = pl.BlockSpec(memory_space=pltpu.VMEM)
    hbm = pl.BlockSpec(memory_space=pl.ANY)
    smem = pl.BlockSpec(memory_space=pltpu.SMEM)
    return pl.pallas_call(
        functools.partial(near_kernel, size_x, size_y),
        out_shape=(
            jax.ShapeDtypeStruct((leaf_dev - border, width), jnp.float32),
            jax.ShapeDtypeStruct((border, width), jnp.float32),
            jax.ShapeDtypeStruct((border, width), jnp.float32),
            jax.ShapeDtypeStruct((1,), jnp.int32),
            jax.ShapeDtypeStruct((12 * places * border, width), jnp.bfloat16),
            jax.ShapeDtypeStruct((places, *pairs.shape), jnp.int32),
        ),
        in_specs=[hbm] * 6,
        out_specs=(hbm, vmem, vmem, smem, hbm, hbm),
        scratch_shapes=[
            pltpu.VMEM(coef.shape, coef.dtype),
            pltpu.VMEM(pairs.shape, jnp.int32),
            pltpu.VMEM(level.shape, jnp.int32),
            pltpu.VMEM(inner_list.shape, jnp.int32),
            pltpu.VMEM(inner_class.shape, jnp.int32),
            pltpu.VMEM((classes, width, width), jnp.bfloat16),
            pltpu.VMEM((classes * leaf_dev * ROWS, 128), jnp.float32),
            pltpu.VMEM((leaf_dev * ROWS, 128), jnp.float32),
            pltpu.VMEM((leaf_dev, width), jnp.float32),
            pltpu.VMEM(inner_list.shape, jnp.int32),
            pltpu.SMEM((SLOTS, inner_list.shape[0], 128), jnp.int32),
            pltpu.VMEM((places * border, width), jnp.bfloat16),
            pltpu.VMEM((places, *pairs.shape), jnp.int32),
            pltpu.VMEM((slots, places * border), jnp.bfloat16),
            pltpu.VMEM((slots, border), jnp.float32),
            pltpu.VMEM((slots, width), jnp.bfloat16),
            pltpu.VMEM((own, width), jnp.bfloat16),
            pltpu.VMEM((slots, width), jnp.float32),
            pltpu.VMEM((own, width), jnp.float32),
            pltpu.SemaphoreType.DMA((classes,)),
            pltpu.SemaphoreType.DMA((2, places)),
            pltpu.SemaphoreType.DMA((2, places)),
            pltpu.SemaphoreType.DMA((2,)),
            pltpu.SemaphoreType.DMA((1,)),
            pltpu.SemaphoreType.DMA((SLOTS,)),
            pltpu.SemaphoreType.DMA((5,)),
        ],
        compiler_params=pltpu.CompilerParams(
            collective_id=0, has_side_effects=True, vmem_limit_bytes=54 << 20
        ),
    )(coef, pairs, level, inner_list, inner_class, tables)


def finish_kernel(
    size_x,
    size_y,
    most,
    rest,
    fast,
    inner,
    halo_hbm,
    lists_hbm,
    pairs_hbm,
    level_hbm,
    tabs_hbm,
    out,
    halo,
    lists,
    pairs,
    level,
    table,
    total,
    final,
    whole,
    sem,
):
    border, width = total.shape
    own = pairs.shape[1]
    leaf_dev = out.shape[0]
    pieces = leaf_dev // border

    def piece(i):
        return pl.ds(i * border, border)

    taken = [
        pltpu.make_async_copy(rest.at[piece(i - 1)] if i else fast, whole.at[piece(i)], sem.at[0, i])
        for i in range(pieces)
    ]
    given = [pltpu.make_async_copy(whole.at[piece(i)], out.at[piece(i)], sem.at[1, i]) for i in range(pieces)]
    for copy in taken:
        copy.start()
    for copy, onward in zip(taken, given, strict=True):
        copy.wait()
        onward.start()
    for copy in given:
        copy.wait()

    @pl.when(most[0] >= ROOM)
    def _():
        def bring(source, target):
            copy = pltpu.make_async_copy(source, target, sem.at[0, 0])
            copy.start()
            copy.wait()

        bring(halo_hbm.at[pl.ds(0, halo.shape[0])], halo)
        bring(lists_hbm, lists)
        bring(pairs_hbm, pairs)
        bring(level_hbm, level)
        my_x, my_y = lax.axis_index("gx"), lax.axis_index("gy")
        rank = my_x * size_y + my_y

        def add(row, kind, at, times):
            line = iota((128, own), 0)
            columns = jnp.transpose(jnp.where(line == 0, row, kind).astype(jnp.float32))
            row_col = columns[:, 0:1].astype(jnp.int32)
            kind_col = columns[:, 1:2].astype(jnp.int32)
            rows = dot(one_hot(iota((own, halo.shape[0]), 1) == row_col), halo[...])
            picks = one_hot(iota((border, own), 0) == at)

            def class_step(c, _):
                bring(tabs_hbm.at[c], table)
                for part in split(times(jnp.where(kind_col == c, rows, 0.0).astype(jnp.bfloat16), table[...])):
                    total[...] += dot(picks, part)
                return 0

            lax.fori_loop(0, tabs_hbm.shape[0], class_step, 0)

        total[...] = jnp.zeros_like(total)
        target, source, kind = pairs[0:1, :], pairs[1:2, :], pairs[2:3, :]
        home = source // leaf_dev
        place = place_of(home // size_y - my_x, home % size_y - my_y)
        add(place * border + source % leaf_dev, kind, target - rank * leaf_dev, dot)

        def list_step(o, _):
            row = o * border + lists[o, 0:1, :] % leaf_dev
            add(row, lists[o, 2:3, :], lists[o, 1:2, :] - rank * leaf_dev, dot_t)
            return 0

        lax.fori_loop(0, lists.shape[0], list_step, 0)
        bring(inner, final)
        by = down(scale_of(level[...]), 0)
        for j in range(width // 128):
            lanes = slice(128 * j, 128 * j + 128)
            final[:, lanes] = final[:, lanes] + total[:, lanes] * by
        bring(final, out.at[pl.ds(0, border)])


def finish(size_x, size_y, most, rest, fast, inner, halo, lists, pairs, level, tables):
    border, width = fast.shape
    hbm = pl.BlockSpec(memory_space=pl.ANY)
    return pl.pallas_call(
        functools.partial(finish_kernel, size_x, size_y),
        out_shape=jax.ShapeDtypeStruct((rest.shape[0] + border, width), jnp.float32),
        in_specs=[pl.BlockSpec(memory_space=pltpu.SMEM)] + [hbm] * 8,
        out_specs=hbm,
        scratch_shapes=[
            pltpu.VMEM((len(STEPS) * border, width), jnp.bfloat16),
            pltpu.VMEM(lists.shape, jnp.int32),
            pltpu.VMEM(pairs.shape, jnp.int32),
            pltpu.VMEM(level.shape, jnp.int32),
            pltpu.VMEM(tables.shape[1:], jnp.bfloat16),
            pltpu.VMEM((border, width), jnp.float32),
            pltpu.VMEM((border, width), jnp.float32),
            pltpu.VMEM((rest.shape[0] + border, width), jnp.float32),
            pltpu.SemaphoreType.DMA((2, rest.shape[0] // border + 1)),
        ],
        compiler_params=pltpu.CompilerParams(vmem_limit_bytes=60 << 20),
    )(most, rest, fast, inner, halo, lists, pairs, level, tables)


def body(coef, tables, leaf_level, inner_list, inner_class, cross_pairs):
    leaf_dev, width = coef.shape
    size_x, size_y = lax.axis_size("gx"), lax.axis_size("gy")
    level = leaf_level.reshape(leaf_dev // 128, 128)
    rest, fast, inner, most, halo, lists = near_parts(
        size_x, size_y, coef, tables, cross_pairs, level, inner_list.T, inner_class.T
    )

    return finish(size_x, size_y, most, rest, fast, inner, halo, lists, cross_pairs, level, tables)


def solution(mesh):
    return jax.shard_map(
        body,
        mesh=mesh,
        in_specs=(
            P(("gx", "gy"), None),
            P(),
            P(("gx", "gy")),
            P(("gx", "gy"), None),
            P(("gx", "gy"), None),
            P(None, ("gx", "gy")),
        ),
        out_specs=P(("gx", "gy"), None),
        check_vma=False,
    )
```

```python
import functools

import jax
import jax.numpy as jnp
from jax import lax
from jax.experimental import pallas as pl
from jax.experimental.pallas import tpu as pltpu
from jax.sharding import PartitionSpec as P

MESH = pl.DeviceIdType.MESH
ROWS = 4
ROOM = 64
FIRST = 6
SLOTS = 4
STEPS = [(-1, -1), (-1, 0), (-1, 1), (1, -1), (1, 0), (1, 1), (0, -1), (0, 1)]


def place_of(dx, dy):
    if isinstance(dx, int):
        return {-1: dy + 1, 1: dy + 4, 0: 6 + (dy + 1) // 2}[dx]
    return jnp.where(dx < 0, dy + 1, jnp.where(dx > 0, dy + 4, 6 + (dy + 1) // 2))


def dot(a, b):
    return jnp.dot(a, b, preferred_element_type=jnp.float32)


def dot_t(a, b):
    return lax.dot_general(a, b, (((1,), (1,)), ((), ())), preferred_element_type=jnp.float32)


def split(z):
    high = z.astype(jnp.bfloat16)
    return high, (z - high.astype(jnp.float32)).astype(jnp.bfloat16)


def one_hot(mask):
    return jnp.where(mask, 1.0, 0.0).astype(jnp.bfloat16)


def iota(shape, dim):
    return lax.broadcasted_iota(jnp.int32, shape, dim)


def scale_of(levels):
    scale = jnp.ones(levels.shape, jnp.float32)
    for bit in range(3):
        scale = scale * jnp.where((levels & (1 << bit)) != 0, 0.25 ** (1 << bit), 1.0)
    return scale


def down(scale, a):
    return jnp.transpose(jnp.broadcast_to(scale[a : a + 1, :], (128, 128)))


def near_kernel(
    size_x,
    size_y,
    coef_hbm,
    pairs_hbm,
    level_hbm,
    inner_list_hbm,
    inner_class_hbm,
    tabs_hbm,
    rest_out,
    border_out,
    inner_out,
    most_out,
    halo_out,
    lists_out,
    coef,
    pairs,
    level,
    inner_list,
    inner_class,
    tabs,
    y,
    acc,
    out,
    idx,
    idx_slot,
    halo,
    lists,
    g,
    back,
    x_m,
    x_f,
    z_m,
    z_f,
    tab_sem,
    send_sem,
    recv_sem,
    save_sem,
    out_sem,
    idx_sem,
    arg_sem,
):
    leaf_dev, width = coef.shape
    classes = tabs.shape[0]
    border = leaf_dev // 8
    own = pairs.shape[1]
    my_x, my_y = lax.axis_index("gx"), lax.axis_index("gy")

    def table_copy(c):
        return pltpu.make_async_copy(tabs_hbm.at[c], tabs.at[c], tab_sem.at[c])

    arguments = [
        pltpu.make_async_copy(source, target, arg_sem.at[i])
        for i, (source, target) in enumerate(
            (
                (coef_hbm, coef),
                (pairs_hbm, pairs),
                (level_hbm, level),
                (inner_list_hbm, inner_list),
                (inner_class_hbm, inner_class),
            )
        )
    ]
    arguments[0].start()
    for c in range(2):
        table_copy(c).start()
    for argument in arguments[1:]:
        argument.start()
    for c in range(2, classes):
        table_copy(c).start()

    def neighbour(dx, dy):
        return lax.rem(my_x + dx + size_x, size_x), lax.rem(my_y + dy + size_y, size_y)

    barrier = pltpu.get_barrier_semaphore()
    for dx, dy in STEPS:
        pl.semaphore_signal(barrier, inc=1, device_id=neighbour(dx, dy), device_id_type=MESH)

    def idx_copy(chunk, slot):
        lanes = pl.ds(pl.multiple_of(chunk * 128, 128), 128)
        return pltpu.make_async_copy(idx.at[:, lanes], idx_slot.at[slot], idx_sem.at[slot])

    def tables_step(i, _):
        for u in range(2):
            c = i * 2 + u
            table_copy(c).wait()
            half = leaf_dev // 2
            for m in range(0, leaf_dev, half):
                r = dot(coef[m : m + half, :], tabs[c])
                for j in range(ROWS):
                    y[pl.ds(c * (ROWS * leaf_dev) + (ROWS * m + j), half, stride=ROWS), :] = r[
                        :, 128 * j : 128 * j + 128
                    ]
        return 0

    arguments[0].wait()
    lax.fori_loop(0, FIRST // 2, tables_step, 0)
    for argument in arguments[1:]:
        argument.wait()
    pl.semaphore_wait(barrier, len(STEPS))
    mate = 1 - 2 * lax.rem(my_y, 2)

    def rows_of(place):
        return halo.at[pl.ds(place * border, border)]

    def halo_copy(source, sent, place, dx, dy):
        return pltpu.make_async_remote_copy(
            src_ref=source,
            dst_ref=rows_of(place),
            send_sem=send_sem.at[0, sent],
            recv_sem=recv_sem.at[0, place],
            device_id=neighbour(dx, dy),
            device_id_type=MESH,
        )

    list_copies = []
    for there, (dx, dy) in enumerate(STEPS):
        copy = pltpu.make_async_remote_copy(
            src_ref=pairs,
            dst_ref=lists.at[place_of(-dx, -dy)],
            send_sem=send_sem.at[1, there],
            recv_sem=recv_sem.at[1, place_of(-dx, -dy)],
            device_id=neighbour(dx, dy),
            device_id_type=MESH,
        )
        copy.start()
        list_copies.append(copy)
    mine = coef.at[pl.ds(0, border)]
    sends = [(-1, 0), (1, 0), (0, -mate), (-1, -mate), (1, -mate), (0, mate)]
    halo_copies = [
        halo_copy(mine, sent, place_of(-dx, -dy), dx, dy) for sent, (dx, dy) in enumerate(sends)
    ]
    for copy in halo_copies:
        copy.start()
    idx[...] = ((inner_class[...] & (classes - 1)) * leaf_dev + (inner_list[...] & (leaf_dev - 1))) * ROWS
    for slot in range(SLOTS):
        idx_copy(slot, slot).start()
    lax.fori_loop(FIRST // 2, classes // 2, tables_step, 0)

    def leaf_step(i, _):
        for slot in range(SLOTS):
            chunk = i * SLOTS + slot
            idx_copy(chunk, slot).wait()
            for u in range(128):
                total = None
                for k in range(8):
                    v = y[pl.ds(idx_slot[slot, k, u], ROWS), :]
                    total = v if total is None else total + v
                acc[pl.ds(chunk * (128 * ROWS) + u * ROWS, ROWS), :] = total

            idx_copy(lax.rem(chunk + SLOTS, leaf_dev // 128), slot).start()
        return 0

    lax.fori_loop(0, leaf_dev // 128 // SLOTS, leaf_step, 0)
    for slot in range(SLOTS):
        idx_copy(slot, slot).wait()

    scale = scale_of(level[...])

    for a in range(leaf_dev // 128):
        by = down(scale, a)
        for j in range(ROWS):
            rows = acc[pl.ds(a * 128 * ROWS + j, 128, stride=ROWS), :] * by
            out[a * 128 : a * 128 + 128, 128 * j : 128 * j + 128] = rows
    rest_copy = pltpu.make_async_copy(
        out.at[pl.ds(border, leaf_dev - border)], rest_out, out_sem.at[0]
    )
    rest_copy.start()

    for sent, dx in ((6, -1), (7, 1)):
        came = place_of(dx, 0)
        halo_copy(rows_of(came), sent, came, 0, mate).wait_recv()
        copy = halo_copy(rows_of(came), sent, place_of(dx, -mate), 0, mate)
        copy.start()
        halo_copies.append(copy)
    for copy in list_copies:
        copy.wait()
    target, source, kind = pairs[0:1, :], pairs[1:2, :], pairs[2:3, :]
    rank = my_x * size_y + my_y
    home = source // leaf_dev
    place = place_of(home // size_y - my_x, home % size_y - my_y)
    row = place * border + source % leaf_dev
    line = iota((128, own), 0)
    columns = jnp.transpose(jnp.where(line == 0, row, kind).astype(jnp.float32))
    row_col = columns[:, 0:1].astype(jnp.int32)
    kind_col = columns[:, 1:2].astype(jnp.int32)
    picker = one_hot(iota((own, halo.shape[0]), 1) == row_col)

    slots = classes * ROOM
    earlier = one_hot(iota((own, own), 0) < iota((own, own), 1))
    back[...] = jnp.zeros_like(back)

    before = jnp.zeros((classes, 1), jnp.float32)
    most = jnp.zeros((1, own), jnp.int32)
    for o in range(len(STEPS)):
        from_leaf = lists[o, 0:1, :] % leaf_dev
        to_leaf = lists[o, 1:2, :] - rank * leaf_dev
        o_kind = lists[o, 2:3, :]
        here = (to_leaf >= 0) & (to_leaf < border)
        kinds = one_hot((iota((classes, own), 0) == o_kind) & here)
        ahead = dot(kinds, earlier) + before
        hits = kinds.astype(jnp.float32)
        place_in = jnp.sum(ahead * hits, axis=0, keepdims=True).astype(jnp.int32)
        most = jnp.maximum(most, jnp.where(here, place_in, 0))
        room = one_hot(iota((ROOM, own), 0) == place_in)
        e = jnp.concatenate([room * kinds[c : c + 1, :] for c in range(classes)], axis=0)
        lines = iota((2 * border, own), 0)
        w = one_hot(lines == jnp.where(lines < border, from_leaf, to_leaf + border))
        both = dot_t(e, w)
        g[:, o * border : (o + 1) * border] = both[:, :border].astype(jnp.bfloat16)
        back[...] += both[:, border:]
        before = before + jnp.sum(hits, axis=1, keepdims=True)
    most_out[0] = jnp.max(most)
    to_target = one_hot(iota((border, own), 0) == target - rank * leaf_dev)
    to_source = jnp.transpose(back[...]).astype(jnp.bfloat16)
    for copy in halo_copies:
        copy.wait_send()
    for place in range(len(STEPS)):
        if place not in (place_of(-1, 0), place_of(1, 0)):
            halo_copy(rows_of(place), 0, place, 0, mate).wait_recv()
    saves = [
        pltpu.make_async_copy(halo, halo_out.at[pl.ds(0, halo.shape[0])], save_sem.at[0]),
        pltpu.make_async_copy(lists, lists_out, save_sem.at[1]),
    ]
    for save in saves:
        save.start()
    x_f[...] = dot(picker, halo[...]).astype(jnp.bfloat16)
    x_m[...] = dot(g[...], halo[...]).astype(jnp.bfloat16)


    for c in range(classes):
        rows = jnp.where(kind_col == c, x_f[...].astype(jnp.float32), 0.0).astype(jnp.bfloat16)
        part = dot(rows, tabs[c])
        z_f[...] = part if c == 0 else z_f[...] + part
        z_m[c * ROOM : (c + 1) * ROOM, :] = dot_t(x_m[c * ROOM : (c + 1) * ROOM, :], tabs[c])

    border_sum = None
    for picks, z in ((to_target, z_f[...]), (to_source, z_m[...])):
        for part in split(z):
            term = dot(picks, part)
            border_sum = term if border_sum is None else border_sum + term
    inner_out[...] = out[0:border, :]
    by = down(scale, 0)
    for j in range(ROWS):
        lanes = slice(128 * j, 128 * j + 128)
        border_out[:, lanes] = out[0:border, lanes] + border_sum[:, lanes] * by
    for save in (*saves, rest_copy):
        save.wait()


def near_parts(size_x, size_y, coef, tables, pairs, level, inner_list, inner_class):
    leaf_dev, width = coef.shape
    classes = tables.shape[0]
    border = leaf_dev // 8
    own = pairs.shape[1]
    places = len(STEPS)
    slots = classes * ROOM
    vmem = pl.BlockSpec(memory_space=pltpu.VMEM)
    hbm = pl.BlockSpec(memory_space=pl.ANY)
    smem = pl.BlockSpec(memory_space=pltpu.SMEM)
    return pl.pallas_call(
        functools.partial(near_kernel, size_x, size_y),
        out_shape=(
            jax.ShapeDtypeStruct((leaf_dev - border, width), jnp.float32),
            jax.ShapeDtypeStruct((border, width), jnp.float32),
            jax.ShapeDtypeStruct((border, width), jnp.float32),
            jax.ShapeDtypeStruct((1,), jnp.int32),
            jax.ShapeDtypeStruct((12 * places * border, width), jnp.bfloat16),
            jax.ShapeDtypeStruct((places, *pairs.shape), jnp.int32),
        ),
        in_specs=[hbm] * 6,
        out_specs=(hbm, vmem, vmem, smem, hbm, hbm),
        scratch_shapes=[
            pltpu.VMEM(coef.shape, coef.dtype),
            pltpu.VMEM(pairs.shape, jnp.int32),
            pltpu.VMEM(level.shape, jnp.int32),
            pltpu.VMEM(inner_list.shape, jnp.int32),
            pltpu.VMEM(inner_class.shape, jnp.int32),
            pltpu.VMEM((classes, width, width), jnp.bfloat16),
            pltpu.VMEM((classes * leaf_dev * ROWS + 8, 128), jnp.float32),
            pltpu.VMEM((leaf_dev * ROWS + 8, 128), jnp.float32),
            pltpu.VMEM((leaf_dev, width), jnp.float32),
            pltpu.VMEM(inner_list.shape, jnp.int32),
            pltpu.SMEM((SLOTS, inner_list.shape[0], 128), jnp.int32),
            pltpu.VMEM((places * border, width), jnp.bfloat16),
            pltpu.VMEM((places, *pairs.shape), jnp.int32),
            pltpu.VMEM((slots, places * border), jnp.bfloat16),
            pltpu.VMEM((slots, border), jnp.float32),
            pltpu.VMEM((slots, width), jnp.bfloat16),
            pltpu.VMEM((own, width), jnp.bfloat16),
            pltpu.VMEM((slots, width), jnp.float32),
            pltpu.VMEM((own, width), jnp.float32),
            pltpu.SemaphoreType.DMA((classes,)),
            pltpu.SemaphoreType.DMA((2, places)),
            pltpu.SemaphoreType.DMA((2, places)),
            pltpu.SemaphoreType.DMA((2,)),
            pltpu.SemaphoreType.DMA((1,)),
            pltpu.SemaphoreType.DMA((SLOTS,)),
            pltpu.SemaphoreType.DMA((5,)),
        ],
        compiler_params=pltpu.CompilerParams(
            collective_id=0, has_side_effects=True, vmem_limit_bytes=54 << 20
        ),
    )(coef, pairs, level, inner_list, inner_class, tables)


def finish_kernel(
    size_x,
    size_y,
    most,
    rest,
    fast,
    inner,
    halo_hbm,
    lists_hbm,
    pairs_hbm,
    level_hbm,
    tabs_hbm,
    out,
    halo,
    lists,
    pairs,
    level,
    table,
    total,
    final,
    whole,
    sem,
):
    border, width = total.shape
    own = pairs.shape[1]
    leaf_dev = out.shape[0]
    pieces = leaf_dev // border

    def piece(i):
        return pl.ds(i * border, border)

    taken = [
        pltpu.make_async_copy(rest.at[piece(i - 1)] if i else fast, whole.at[piece(i)], sem.at[0, i])
        for i in range(pieces)
    ]
    given = [pltpu.make_async_copy(whole.at[piece(i)], out.at[piece(i)], sem.at[1, i]) for i in range(pieces)]
    for copy in taken:
        copy.start()
    for copy, onward in zip(taken, given, strict=True):
        copy.wait()
        onward.start()
    for copy in given:
        copy.wait()

    @pl.when(most[0] >= ROOM)
    def _():
        def bring(source, target):
            copy = pltpu.make_async_copy(source, target, sem.at[0, 0])
            copy.start()
            copy.wait()

        bring(halo_hbm.at[pl.ds(0, halo.shape[0])], halo)
        bring(lists_hbm, lists)
        bring(pairs_hbm, pairs)
        bring(level_hbm, level)
        my_x, my_y = lax.axis_index("gx"), lax.axis_index("gy")
        rank = my_x * size_y + my_y

        def add(row, kind, at, times):
            line = iota((128, own), 0)
            columns = jnp.transpose(jnp.where(line == 0, row, kind).astype(jnp.float32))
            row_col = columns[:, 0:1].astype(jnp.int32)
            kind_col = columns[:, 1:2].astype(jnp.int32)
            rows = dot(one_hot(iota((own, halo.shape[0]), 1) == row_col), halo[...])
            picks = one_hot(iota((border, own), 0) == at)

            def class_step(c, _):
                bring(tabs_hbm.at[c], table)
                for part in split(times(jnp.where(kind_col == c, rows, 0.0).astype(jnp.bfloat16), table[...])):
                    total[...] += dot(picks, part)
                return 0

            lax.fori_loop(0, tabs_hbm.shape[0], class_step, 0)

        total[...] = jnp.zeros_like(total)
        target, source, kind = pairs[0:1, :], pairs[1:2, :], pairs[2:3, :]
        home = source // leaf_dev
        place = place_of(home // size_y - my_x, home % size_y - my_y)
        add(place * border + source % leaf_dev, kind, target - rank * leaf_dev, dot)

        def list_step(o, _):
            row = o * border + lists[o, 0:1, :] % leaf_dev
            add(row, lists[o, 2:3, :], lists[o, 1:2, :] - rank * leaf_dev, dot_t)
            return 0

        lax.fori_loop(0, lists.shape[0], list_step, 0)
        bring(inner, final)
        by = down(scale_of(level[...]), 0)
        for j in range(width // 128):
            lanes = slice(128 * j, 128 * j + 128)
            final[:, lanes] = final[:, lanes] + total[:, lanes] * by
        bring(final, out.at[pl.ds(0, border)])


def finish(size_x, size_y, most, rest, fast, inner, halo, lists, pairs, level, tables):
    border, width = fast.shape
    hbm = pl.BlockSpec(memory_space=pl.ANY)
    return pl.pallas_call(
        functools.partial(finish_kernel, size_x, size_y),
        out_shape=jax.ShapeDtypeStruct((rest.shape[0] + border, width), jnp.float32),
        in_specs=[pl.BlockSpec(memory_space=pltpu.SMEM)] + [hbm] * 8,
        out_specs=hbm,
        scratch_shapes=[
            pltpu.VMEM((len(STEPS) * border, width), jnp.bfloat16),
            pltpu.VMEM(lists.shape, jnp.int32),
            pltpu.VMEM(pairs.shape, jnp.int32),
            pltpu.VMEM(level.shape, jnp.int32),
            pltpu.VMEM(tables.shape[1:], jnp.bfloat16),
            pltpu.VMEM((border, width), jnp.float32),
            pltpu.VMEM((border, width), jnp.float32),
            pltpu.VMEM((rest.shape[0] + border, width), jnp.float32),
            pltpu.SemaphoreType.DMA((2, rest.shape[0] // border + 1)),
        ],
        compiler_params=pltpu.CompilerParams(vmem_limit_bytes=60 << 20),
    )(most, rest, fast, inner, halo, lists, pairs, level, tables)


def body(coef, tables, leaf_level, inner_list, inner_class, cross_pairs):
    leaf_dev, width = coef.shape
    size_x, size_y = lax.axis_size("gx"), lax.axis_size("gy")
    level = leaf_level.reshape(leaf_dev // 128, 128)
    rest, fast, inner, most, halo, lists = near_parts(
        size_x, size_y, coef, tables, cross_pairs, level, inner_list.T, inner_class.T
    )

    return finish(size_x, size_y, most, rest, fast, inner, halo, lists, cross_pairs, level, tables)


def solution(mesh):
    return jax.shard_map(
        body,
        mesh=mesh,
        in_specs=(
            P(("gx", "gy"), None),
            P(),
            P(("gx", "gy")),
            P(("gx", "gy"), None),
            P(("gx", "gy"), None),
            P(None, ("gx", "gy")),
        ),
        out_specs=P(("gx", "gy"), None),
        check_vma=False,
    )
```
